512 devices in a mesh: seq: 32 (over z, core), cp: 16 (over x, y).
Axes of the slice: x: 4, y: 4, z: 16, core: 2. Of those that a mesh axis runs over, the one named last changes fastest.
Arguments:
- queries: bfloat16 [65536, 768], P(('seq', 'cp')), parts along dimension 0, may hold values from -6 to 6, as said below
- keys: bfloat16 [65536, 128], P(('seq', 'cp')), parts along dimension 0, may hold values from -6 to 6, as said below
- values: bfloat16 [65536, 128], P(('seq', 'cp')), parts along dimension 0, may hold values from -6 to 6
- out_grad: bfloat16 [65536, 768], P(('seq', 'cp')), parts along dimension 0, may hold values from -6 to 6
- positions: int32 [3, 65536], P(None, 'seq'), parts along dimension 1, may hold values from 0 to 2047
- doc_ids: int32 [65536], P('seq'), parts along dimension 0, may hold values from 0 to 7, never falling along the last dimension, each value on 1 to 1024 neighbouring positions
- stretch_order: int32 [1024], P('seq'), parts along dimension 0, may hold values from 0 to 31, each once
Outputs:
- attn_out: bfloat16 [65536, 768], P(('seq', 'cp')), parts along dimension 0
- grad_queries: bfloat16 [65536, 768], P(('seq', 'cp')), parts along dimension 0
- grad_keys: bfloat16 [65536, 128], P(('seq', 'cp')), parts along dimension 0
- grad_values: bfloat16 [65536, 128], P(('seq', 'cp')), parts along dimension 0
The draws below stay inside these ranges and needn't reach their ends.
There are 32 independent parts, one for each index of `seq`. The reference program is written for one: setup_inputs(seed, part) draws one part's arguments, and reference() takes and returns one part's arrays. A program takes and returns all parts, laid end to end along the dimension named above; each array names one. Nothing has to cross between parts.
Inputs may be any that keep to these rules, and one draw needn't show every extreme that they name: `queries`: values of one part; a few tokens may have large entries. `keys`: values of one part; a few tokens may have large entries. `doc_ids`: never falls along the sequence; each document holds at most 1024 tokens. `stretch_order`: each block number appears once.
All inputs are finite; a program needn't handle non-finite values.
Results may differ from the reference program's by a relative error of at most 0.01.
Values may be sent and summed in bfloat16 or wider, within the bound.
No kernel may reach another device: no remote copies, remote signals or barrier semaphores. Data moves between devices by JAX's collectives and lax.ppermute only.
A program may use at most 64 MiB of HBM per device.

```python
import math
import jax
import jax.numpy as jnp
import numpy as np
from jax import lax

HQ = 6
HK = 1
HD = 128
DOCS = 8
GROUP = 6
SEC_T = 16
SEC_H = 24
STRETCH = 64
STRETCHES = 32
SEQ_LEN = 2048


def draw_keys(key, part):
    base = jnp.clip(jax.random.normal(jax.random.fold_in(key, 1), (SEQ_LEN, HK * HD)), -6.0, 6.0)
    return base.astype(jnp.bfloat16)


def draw_queries(key, part):
    base = jnp.clip(jax.random.normal(jax.random.fold_in(key, 2), (SEQ_LEN, HQ * HD)), -6.0, 6.0)
    return base.astype(jnp.bfloat16)


def set_ends(entries, stream_key, low, high):
    place = [jax.random.randint(jax.random.fold_in(stream_key, axis), (), 0, length) for axis, length in enumerate(entries.shape)]
    main_axis = entries.shape.index(max(entries.shape))
    next_to = place[:main_axis] + [(place[main_axis] + 1) % entries.shape[main_axis]] + place[main_axis + 1:]
    return entries.at[tuple(place)].set(low).at[tuple(next_to)].set(high)


def block_levels(rng, shape, shards, smallest, largest):
    loudness = 1.0
    for dim, blocks in shards:
        steps = jax.random.uniform(jax.random.fold_in(jax.random.fold_in(rng, 6), dim), (blocks,), jnp.float32, smallest / len(shards), largest / len(shards))
        loudness = loudness * jnp.repeat(jnp.exp(steps), shape[dim] // blocks).reshape((-1,) + (1,) * (len(shape) - 1 - dim))
    return loudness


def length_profile(amount, total, bound, slope):
    weights = [(1 << 20) // math.isqrt(grade ** slope) + 1 for grade in range(2, amount + 1)]
    spare, given = total - bound - (amount - 1), [1] * (amount - 1)
    while spare > 0:
        candidates = [i for i in range(amount - 1) if given[i] < bound]
        mass, budget = sum([weights[i] for i in candidates]), spare
        for i in candidates:
            addition = min(bound - given[i], max(1, budget * weights[i] // mass), spare)
            given[i] = given[i] + addition
            spare = spare - addition
    return np.array([bound] + given)


def ragged_sizes(stream_key, number_of, total, bound, skew):
    if number_of == 2:
        one = jax.random.randint(stream_key, (), max(1, total - bound), min(bound, total - 1) + 1)
        return jnp.stack([one, total - one])
    sizes = jnp.asarray(length_profile(number_of, total, bound, skew), jnp.int32)
    pairs = (number_of - 1) // 2
    donor, sink = sizes[1:1 + 2 * pairs:2], sizes[2:2 + 2 * pairs:2]
    margin = jnp.minimum(donor - 1, bound - sink)
    shifted = jax.random.randint(jax.random.fold_in(stream_key, 1), (pairs,), 0, 1 << 20) % (margin + 1)
    sizes = sizes.at[1:1 + 2 * pairs:2].set(donor - shifted).at[2:2 + 2 * pairs:2].set(sink + shifted)
    return sizes[jax.random.permutation(jax.random.fold_in(stream_key, 2), number_of)]


def normal_values(own_key, extent, deviation, most, split=(), kind=jnp.bfloat16):
    loudness = block_levels(own_key, extent, split, -0.22, 0.18) if split else 1.0
    values = jax.random.normal(own_key, extent, jnp.float32) * deviation * loudness
    return jnp.minimum(jnp.maximum(values, -most), most).astype(kind)


def setup_inputs(seed: int = 0, part: int = 0) -> dict:
    arg_keys = jax.random.split(jax.random.key(seed), 8)
    part_keys = jax.random.split(jax.random.fold_in(arg_keys[7], part), 8)
    queries = draw_queries(jax.random.fold_in(jax.random.fold_in(arg_keys[7], part), 71), part)
    keys = draw_keys(jax.random.fold_in(jax.random.fold_in(arg_keys[7], part), 71), part)
    values = normal_values(part_keys[2], (SEQ_LEN, HK * HD), 1.0, 6.0, ((0, 16),))
    out_grad = normal_values(part_keys[3], (SEQ_LEN, HQ * HD), 1.0, 6.0, ((0, 16),))
    positions = set_ends(jax.random.randint(part_keys[4], (3, SEQ_LEN), 0, SEQ_LEN), jax.random.fold_in(part_keys[4], 1), 0, SEQ_LEN - 1).astype(jnp.int32)
    doc_ids = jnp.searchsorted(jnp.cumsum(ragged_sizes(part_keys[5], DOCS, SEQ_LEN, SEQ_LEN // 2, 2)), jnp.arange(SEQ_LEN), side="right").astype(jnp.int32)
    stretch_order = jax.random.permutation(part_keys[6], STRETCHES).astype(jnp.int32)
    return {"queries": queries, "keys": keys, "values": values, "out_grad": out_grad, "positions": positions, "doc_ids": doc_ids, "stretch_order": stretch_order}


def rotary_tables(pos3):
    half = HD // 2
    pairs = jnp.arange(half, dtype=jnp.int32)
    freqs = jnp.exp(-(2.0 * pairs.astype(jnp.float32) / HD) * math.log(1000000.0))
    pos_f = pos3.astype(jnp.float32)
    chosen = jnp.where((pairs < SEC_T)[None, :], pos_f[0][:, None], jnp.where((pairs < SEC_T + SEC_H)[None, :], pos_f[1][:, None], pos_f[2][:, None]))
    angle = chosen * freqs[None, :]
    cosine = jnp.concatenate([jnp.cos(angle), jnp.cos(angle)], axis=1)
    sine_tab = jnp.concatenate([jnp.sin(angle), jnp.sin(angle)], axis=1)
    return (cosine, sine_tab)

def rotate(field, cosine, sine_tab):
    half = HD // 2
    first, second = (field[..., :half], field[..., half:])
    turned = jnp.concatenate([-second, first], axis=-1)
    return field * cosine[:, None, :] + turned * sine_tab[:, None, :]

def rotate_back(field, cosine, sine_tab):
    half = HD // 2
    scaled = field * sine_tab[:, None, :]
    turned = jnp.concatenate([scaled[..., half:], -scaled[..., :half]], axis=-1)
    return field * cosine[:, None, :] + turned

def reference(queries, keys, values, out_grad, positions, doc_ids, stretch_order):
    length = SEQ_LEN
    orig = (stretch_order[:, None] * STRETCH + jnp.arange(STRETCH, dtype=jnp.int32)[None, :]).reshape(length)
    docs = doc_ids[orig]
    cosine, sine_tab = rotary_tables(positions[:, orig])
    q_rot = rotate(queries.astype(jnp.float32).reshape(length, HQ, HD), cosine, sine_tab).astype(jnp.bfloat16)
    k_rot = rotate(keys.astype(jnp.float32).reshape(length, HK, HD), cosine, sine_tab).astype(jnp.bfloat16)
    val_heads = values.reshape(length, HK, HD)
    grad_heads = out_grad.reshape(length, HQ, HD)
    allowed = (docs[:, None] == docs[None, :]) & (orig[None, :] <= orig[:, None])
    score_scale = 1.0 / math.sqrt(HD)
    outputs, dq_list, dk_list, dv_list = ([], [], [], [])
    for group_id in range(HK):
        q_grp = q_rot[:, group_id * GROUP:(group_id + 1) * GROUP, :].astype(jnp.float32)
        k_grp = k_rot[:, group_id, :].astype(jnp.float32)
        v_grp = val_heads[:, group_id, :].astype(jnp.float32)
        do_grp = grad_heads[:, group_id * GROUP:(group_id + 1) * GROUP, :].astype(jnp.float32)
        scores = jnp.einsum('tgd,kd->tgk', q_grp, k_grp) * score_scale
        scores = jnp.where(allowed[:, None, :], scores, -jnp.inf)
        top = lax.optimization_barrier(jnp.max(scores, axis=-1, keepdims=True))
        expo = jnp.exp(scores - top)
        probs32 = expo / lax.optimization_barrier(jnp.sum(expo, axis=-1, keepdims=True))
        probs = probs32.astype(jnp.bfloat16)
        outputs.append(jnp.einsum('tgk,kd->tgd', probs.astype(jnp.float32), v_grp).astype(jnp.bfloat16))
        dprobs = jnp.einsum('tgd,kd->tgk', do_grp, v_grp)
        delta = lax.optimization_barrier(jnp.sum(probs32 * dprobs, axis=-1, keepdims=True))
        dscores = (probs32 * (dprobs - delta)).astype(jnp.bfloat16).astype(jnp.float32)
        dq_list.append(jnp.einsum('tgk,kd->tgd', dscores, k_grp) * score_scale)
        dk_list.append(jnp.einsum('tgk,tgd->kd', dscores, q_grp) * score_scale)
        dv_list.append(jnp.einsum('tgk,tgd->kd', probs.astype(jnp.float32), do_grp))
    attn_out = jnp.concatenate(outputs, axis=1).reshape(length, HQ * HD)
    dq_rot = jnp.concatenate(dq_list, axis=1)
    dk_rot = jnp.stack(dk_list, axis=1)
    grad_queries = rotate_back(dq_rot, cosine, sine_tab).astype(jnp.bfloat16).reshape(length, HQ * HD)
    grad_keys = rotate_back(dk_rot, cosine, sine_tab).astype(jnp.bfloat16).reshape(length, HK * HD)
    grad_values = jnp.stack(dv_list, axis=1).astype(jnp.bfloat16).reshape(length, HK * HD)
    return (attn_out, grad_queries, grad_keys, grad_values)
```

```python
import functools
import math

import jax
import jax.numpy as jnp
from jax import lax
from jax.experimental import pallas as pl
from jax.experimental.pallas import tpu as pltpu
from jax.sharding import PartitionSpec as P

HQ = 6
HD = 128
HALF = HD // 2
SEC_T = 16
SEC_H = 24
STRETCH = 64
DOCS = 8
CHUNK = 256
SUB = 32
LANES = HQ * STRETCH
SCALE = 1.0 / math.sqrt(HD)
LOG2E = math.log2(math.e)

F32 = jnp.float32
BF16 = jnp.bfloat16


def dot_nt(left, right):
    return lax.dot_general(left, right, (((1,), (1,)), ((), ())), preferred_element_type=F32)


def dot_tn(left, right):
    return lax.dot_general(left, right, (((0,), (0,)), ((), ())), preferred_element_type=F32)


def dot_nn(left, right):
    return lax.dot_general(left, right, (((1,), (0,)), ((), ())), preferred_element_type=F32)


def rotated(x, cosine, signed_sine):
    return x * cosine + pltpu.roll(x, HALF, 1) * signed_sine


def rotated_back(x, cosine, signed_sine):
    return x * cosine - pltpu.roll(x, HALF, 1) * signed_sine


def keys_kernel(order_ref, keys_ref, values_ref, pos_ref, payload_ref, cos_ref, sin_ref):
    me = lax.axis_index("cp")
    rows = keys_ref.shape[0]
    lane = lax.broadcasted_iota(jnp.int32, (1, rows), 1)
    windows = []
    for place in range(2):
        stretch = order_ref[2 * me + place]
        start = pl.multiple_of((stretch // 2) * 128, 128)
        window = pos_ref[:, pl.ds(start, 128)].astype(F32)
        turned = pltpu.roll(window, HALF, 1)
        windows.append(jnp.where(stretch % 2 == place, window, turned))
    pos = jnp.where(lane < STRETCH, windows[0], windows[1])
    pair = lax.broadcasted_iota(jnp.int32, (HALF, 1), 0)
    freq = jnp.exp(-(2.0 * pair.astype(F32) / HD) * math.log(1000000.0))
    chosen = jnp.where(
        pair < SEC_T, pos[0:1, :], jnp.where(pair < SEC_T + SEC_H, pos[1:2, :], pos[2:3, :])
    )
    angle = chosen * freq
    table = jnp.concatenate([jnp.cos(angle), jnp.sin(angle)], axis=0).T
    other = pltpu.roll(table, HALF, 1)
    column = lax.broadcasted_iota(jnp.int32, (1, HD), 1)
    cosine = jnp.where(column < HALF, table, other)
    signed_sine = jnp.where(column < HALF, -other, table)
    cos_ref[...] = cosine
    sin_ref[...] = signed_sine
    k_rot = rotated(keys_ref[...].astype(F32), cosine, signed_sine).astype(BF16)
    values = values_ref[...]
    for peer in range(payload_ref.shape[0]):
        payload_ref[peer, :, :HD] = k_rot
        payload_ref[peer, :, HD:] = values


def queries_kernel(queries_ref, grad_ref, cos_ref, sin_ref, docs_ref, q_ref, do_ref, starts_ref):
    for place in range(2):
        rows = pl.ds(place * STRETCH, STRETCH)
        cosine, signed_sine = cos_ref[rows, :], sin_ref[rows, :]
        for head in range(HQ):
            cols = pl.ds(head * HD, HD)
            to = pl.ds(place * LANES + head * STRETCH, STRETCH)
            q_ref[to, :] = rotated(
                queries_ref[rows, cols].astype(F32), cosine, signed_sine
            ).astype(BF16)
            do_ref[to, :] = grad_ref[rows, cols]
    docs = docs_ref[...]
    for doc in range(DOCS):
        starts_ref[doc] = jnp.sum((docs < doc).astype(jnp.int32))


def attention_kernel(
    starts_ref, order_ref, kv_ref, q_ref, do_ref, part_ref, out_ref, dq_ref,
    k_seq, v_seq, s_buf, dp_buf, dk_acc, dv_acc,
):
    me = lax.axis_index("cp")
    blocks = k_seq.shape[0] // STRETCH
    for block in range(blocks):
        to = pl.ds(pl.multiple_of(order_ref[block] * STRETCH, STRETCH), STRETCH)
        rows = pl.ds((block % 2) * STRETCH, STRETCH)
        k_seq[to, :] = kv_ref[block // 2, rows, :HD]
        v_seq[to, :] = kv_ref[block // 2, rows, HD:]
    dk_acc[...] = jnp.zeros_like(dk_acc)
    dv_acc[...] = jnp.zeros_like(dv_acc)
    tiles = LANES // 128
    lane = lax.broadcasted_iota(jnp.int32, (1, 128), 1)
    down = lax.broadcasted_iota(jnp.int32, (SUB, 128), 0)

    def one_stretch(place, carry):
        first = order_ref[2 * me + place] * STRETCH
        token = first + lane % STRETCH
        low = jnp.zeros_like(token)
        lowest = 0
        for doc in range(DOCS):
            start = starts_ref[doc]
            low = jnp.where(start <= token, jnp.maximum(low, start), low)
            lowest = jnp.where(start <= first, jnp.maximum(lowest, start), lowest)
        c_low = lowest // CHUNK
        c_high = first // CHUNK + 1
        mine = pl.ds(pl.multiple_of(place * LANES, LANES), LANES)

        def folded(x, how):
            return how(x.reshape(SUB // 8, 8, 128), axis=0)

        def scores(c, tops):
            at = pl.multiple_of(c * CHUNK, CHUNK)
            s = dot_nt(k_seq[pl.ds(at, CHUNK), :], q_ref[mine, :])
            tops = list(tops)
            for r in range(0, CHUNK, SUB):
                key = down + (at + r)
                allowed = (key >= low) & (key <= token)
                for j in range(tiles):
                    x = jnp.where(allowed, s[r : r + SUB, j * 128 : (j + 1) * 128], -jnp.inf)
                    s_buf[pl.ds(at + r, SUB), j * 128 : (j + 1) * 128] = x
                    tops[j] = jnp.maximum(tops[j], folded(x, jnp.max))
            return tuple(tops)

        tops = lax.fori_loop(
            c_low, c_high, scores, tuple(jnp.full((8, 128), -jnp.inf, F32) for _ in range(tiles))
        )
        factor = SCALE * LOG2E
        tops = [jnp.max(t, axis=0, keepdims=True) * factor for t in tops]

        def weights(c, sums):
            at = pl.multiple_of(c * CHUNK, CHUNK)
            dp = dot_nt(v_seq[pl.ds(at, CHUNK), :], do_ref[mine, :])
            totals, deltas = list(sums[0]), list(sums[1])
            for r in range(0, CHUNK, SUB):
                for j in range(tiles):
                    here = (pl.ds(at + r, SUB), slice(j * 128, (j + 1) * 128))
                    e = jnp.exp2(s_buf[here] * factor - tops[j])
                    d = dp[r : r + SUB, j * 128 : (j + 1) * 128]
                    s_buf[here] = e
                    dp_buf[here] = d
                    totals[j] = totals[j] + folded(e, jnp.sum)
                    deltas[j] = deltas[j] + folded(e * d, jnp.sum)
            return tuple(totals), tuple(deltas)

        zeros = tuple(jnp.zeros((8, 128), F32) for _ in range(tiles))
        totals, deltas = lax.fori_loop(c_low, c_high, weights, (zeros, zeros))
        inverse = [1.0 / jnp.sum(t, axis=0, keepdims=True) for t in totals]
        deltas = [jnp.sum(d, axis=0, keepdims=True) * i for d, i in zip(deltas, inverse)]
        out_ref[place] = jnp.zeros((HD, LANES), F32)
        dq_ref[place] = jnp.zeros((HD, LANES), F32)

        def gradients(c, carry):
            at = pl.multiple_of(c * CHUNK, CHUNK)
            rows = pl.ds(at, CHUNK)
            p_cols, ds_cols = [], []
            for j in range(tiles):
                p_rows, ds_rows = [], []
                for r in range(0, CHUNK, SUB):
                    here = (pl.ds(at + r, SUB), slice(j * 128, (j + 1) * 128))
                    p = s_buf[here] * inverse[j]
                    p_rows.append(p.astype(BF16))
                    ds_rows.append((p * (dp_buf[here] - deltas[j])).astype(BF16))
                p_cols.append(jnp.concatenate(p_rows, axis=0))
                ds_cols.append(jnp.concatenate(ds_rows, axis=0))
            p = jnp.concatenate(p_cols, axis=1)
            ds = jnp.concatenate(ds_cols, axis=1)
            dv_acc[rows, :] += dot_nn(p, do_ref[mine, :])
            dk_acc[rows, :] += dot_nn(ds, q_ref[mine, :])
            out_ref[place] += dot_tn(v_seq[rows, :], p)
            dq_ref[place] += dot_tn(k_seq[rows, :], ds)
            return carry

        lax.fori_loop(c_low, c_high, gradients, 0)
        return carry

    lax.fori_loop(0, 2, one_stretch, 0)
    for block in range(blocks):
        at = pl.ds(pl.multiple_of(order_ref[block] * STRETCH, STRETCH), STRETCH)
        rows = pl.ds((block % 2) * STRETCH, STRETCH)
        part_ref[block // 2, rows, :HD] = (dk_acc[at, :] * SCALE).astype(BF16)
        part_ref[block // 2, rows, HD:] = dv_acc[at, :].astype(BF16)


def outputs_kernel(out_t_ref, dq_t_ref, cos_ref, sin_ref, out_ref, dq_ref):
    for place in range(2):
        rows = pl.ds(place * STRETCH, STRETCH)
        cosine, signed_sine = cos_ref[rows, :], sin_ref[rows, :]
        out = out_t_ref[place].T
        dq = dq_t_ref[place].T
        for head in range(HQ):
            cols = pl.ds(head * HD, HD)
            part = slice(head * STRETCH, (head + 1) * STRETCH)
            out_ref[rows, cols] = out[part].astype(BF16)
            dq_ref[rows, cols] = rotated_back(dq[part] * SCALE, cosine, signed_sine).astype(BF16)


def sums_kernel(parts_ref, cos_ref, sin_ref, dk_ref, dv_ref):
    total = parts_ref[0].astype(F32)
    for peer in range(1, parts_ref.shape[0]):
        total = total + parts_ref[peer].astype(F32)
    dk_ref[...] = rotated_back(total[:, :HD], cos_ref[...], sin_ref[...]).astype(BF16)
    dv_ref[...] = total[:, HD:].astype(BF16)


VMEM = pl.BlockSpec(memory_space=pltpu.VMEM)
SMEM = pl.BlockSpec(memory_space=pltpu.SMEM)


def shards(queries, keys, values, out_grad, positions, doc_ids, stretch_order):
    devices = lax.axis_size("cp")
    rows = queries.shape[0]
    total = rows * devices
    shape = jax.ShapeDtypeStruct
    payload, cosine, signed_sine = pl.pallas_call(
        keys_kernel,
        out_shape=(
            shape((devices, rows, 2 * HD), BF16),
            shape((rows, HD), F32),
            shape((rows, HD), F32),
        ),
        in_specs=[SMEM, VMEM, VMEM, VMEM],
        out_specs=(VMEM, VMEM, VMEM),
        name="keys",
    )(stretch_order, keys, values, positions)
    q_rows, do_rows, starts = pl.pallas_call(
        queries_kernel,
        out_shape=(
            shape((rows * HQ, HD), BF16),
            shape((rows * HQ, HD), BF16),
            shape((DOCS,), jnp.int32),
        ),
        in_specs=[VMEM] * 5,
        out_specs=(VMEM, VMEM, SMEM),
        name="queries",
        cost_estimate=pl.CostEstimate(flops=10**6, transcendentals=0, bytes_accessed=10**6),
    )(queries, out_grad, cosine, signed_sine, doc_ids.reshape(total // 128, 128))
    kv = lax.all_to_all(payload, "cp", 0, 0, tiled=True)
    part, out_t, dq_t = pl.pallas_call(
        attention_kernel,
        out_shape=(
            shape((devices, rows, 2 * HD), BF16),
            shape((2, HD, LANES), F32),
            shape((2, HD, LANES), F32),
        ),
        in_specs=[SMEM, SMEM, VMEM, VMEM, VMEM],
        out_specs=(VMEM, VMEM, VMEM),
        scratch_shapes=[
            pltpu.VMEM((total, HD), BF16),
            pltpu.VMEM((total, HD), BF16),
            pltpu.VMEM((total, LANES), F32),
            pltpu.VMEM((total, LANES), F32),
            pltpu.VMEM((total, HD), F32),
            pltpu.VMEM((total, HD), F32),
        ],
        name="attention",
    )(starts, stretch_order, kv, q_rows, do_rows)
    parts = lax.all_to_all(part, "cp", 0, 0, tiled=True)
    attn_out, grad_queries = pl.pallas_call(
        outputs_kernel,
        out_shape=(shape((rows, HQ * HD), BF16), shape((rows, HQ * HD), BF16)),
        in_specs=[VMEM] * 4,
        out_specs=(VMEM, VMEM),
        name="outputs",
        cost_estimate=pl.CostEstimate(flops=10**6, transcendentals=0, bytes_accessed=10**6),
    )(out_t, dq_t, cosine, signed_sine)
    grad_keys, grad_values = pl.pallas_call(
        sums_kernel,
        out_shape=(shape((rows, HD), BF16), shape((rows, HD), BF16)),
        in_specs=[VMEM] * 3,
        out_specs=(VMEM, VMEM),
        name="sums",
    )(parts, cosine, signed_sine)
    return attn_out, grad_queries, grad_keys, grad_values


def solution(mesh):
    split = P(("seq", "cp"), None)
    return jax.shard_map(
        shards,
        mesh=mesh,
        in_specs=(split, split, split, split, P(None, "seq"), P("seq"), P("seq")),
        out_specs=(split, split, split, split),
        check_vma=False,
    )
```

```python
import math

import jax
import jax.numpy as jnp
from jax import lax
from jax.experimental import pallas as pl
from jax.experimental.pallas import tpu as pltpu
from jax.sharding import PartitionSpec as P

HQ = 6
HD = 128
HALF = HD // 2
SEC_T = 16
SEC_H = 24
STRETCH = 64
DOCS = 8
WINDOW = 1024 + STRETCH
SUB = 32
LANES = HQ * STRETCH
SCALE = 1.0 / math.sqrt(HD)
LOG2E = math.log2(math.e)

F32 = jnp.float32
BF16 = jnp.bfloat16


def dot_nt(left, right):
    return lax.dot_general(left, right, (((1,), (1,)), ((), ())), preferred_element_type=F32)


def dot_tn(left, right):
    return lax.dot_general(left, right, (((0,), (0,)), ((), ())), preferred_element_type=F32)


def dot_nn(left, right):
    return lax.dot_general(left, right, (((1,), (0,)), ((), ())), preferred_element_type=F32)


def rotated(x, cosine, signed_sine):
    return x * cosine + pltpu.roll(x, HALF, 1) * signed_sine


def rotated_back(x, cosine, signed_sine):
    return x * cosine - pltpu.roll(x, HALF, 1) * signed_sine


def expanded(table):
    column = lax.broadcasted_iota(jnp.int32, (1, HD), 1)
    other = pltpu.roll(table, HALF, 1)
    return jnp.where(column < HALF, table, other), jnp.where(column < HALF, -other, table)


def tables_kernel(
    order_ref, pos_ref, docs_ref, queries_ref, grad_ref,
    table_ref, mine_ref, q_ref, do_ref, q_t_ref, do_t_ref, starts_ref,
):
    me = lax.axis_index("cp")
    pair = lax.broadcasted_iota(jnp.int32, (HALF, 1), 0)
    freq = jnp.exp(-(2.0 * pair.astype(F32) / HD) * math.log(1000000.0))

    def some_tokens(c, carry):
        at = pl.ds(pl.multiple_of(c * 128, 128), 128)
        pos = pos_ref[:, at].astype(F32)
        chosen = jnp.where(
            pair < SEC_T, pos[0:1, :], jnp.where(pair < SEC_T + SEC_H, pos[1:2, :], pos[2:3, :])
        )
        angle = chosen * freq
        table_ref[at, :] = jnp.concatenate([jnp.cos(angle), jnp.sin(angle)], axis=0).T
        return carry

    lax.fori_loop(0, pos_ref.shape[1] // 128, some_tokens, 0)
    for place in range(2):
        rows = pl.ds(place * STRETCH, STRETCH)
        first = pl.multiple_of(order_ref[2 * me + place] * STRETCH, STRETCH)
        table = table_ref[pl.ds(first, STRETCH), :]
        mine_ref[rows, :] = table
        cosine, signed_sine = expanded(table)
        for head in range(HQ):
            cols = pl.ds(head * HD, HD)
            to = pl.ds(place * LANES + head * STRETCH, STRETCH)
            q_ref[to, :] = rotated(
                queries_ref[rows, cols].astype(F32), cosine, signed_sine
            ).astype(BF16)
            do_ref[to, :] = grad_ref[rows, cols]
        half = pl.ds(place * LANES, LANES)
        q_t_ref[place] = q_ref[half, :].T
        do_t_ref[place] = do_ref[half, :].T
    docs = docs_ref[...]
    for doc in range(DOCS):
        starts_ref[doc] = jnp.sum((docs < doc).astype(jnp.int32))


def attention_kernel(
    starts_ref, order_ref, kv_ref, table_ref, mine_ref, q_ref, do_ref, q_t_ref, do_t_ref,
    part_ref, out_ref, dq_ref,
    k_seq, v_seq, e_buf, dp_buf, dk_acc, dv_acc, out_buf, dq_buf, sems,
):
    me = lax.axis_index("cp")
    blocks = k_seq.shape[0] // STRETCH
    for block in range(blocks):
        to = pl.ds(pl.multiple_of(order_ref[block] * STRETCH, STRETCH), STRETCH)
        rows = pl.ds((block % 2) * STRETCH, STRETCH)
        k_seq[to, :] = rotated(
            kv_ref[block // 2, rows, :HD].astype(F32), *expanded(table_ref[to, :])
        ).astype(BF16)
        v_seq[to, :] = kv_ref[block // 2, rows, HD:]
    dk_acc[...] = jnp.zeros_like(dk_acc)
    dv_acc[...] = jnp.zeros_like(dv_acc)
    tiles = [slice(j * 128, (j + 1) * 128) for j in range(LANES // 128)]
    steps = range(0, WINDOW, SUB)
    lane = lax.broadcasted_iota(jnp.int32, (1, 128), 1)
    down = lax.broadcasted_iota(jnp.int32, (SUB, 128), 0)
    factor = SCALE * LOG2E

    def folded(x, how):
        return how(x.reshape(SUB // 8, 8, 128), axis=0)

    def one_stretch(place, carry):
        first = order_ref[2 * me + place] * STRETCH
        token = first + lane % STRETCH
        low = jnp.zeros_like(token)
        for doc in range(DOCS):
            start = starts_ref[doc]
            low = jnp.where(start <= token, jnp.maximum(low, start), low)
        base = pl.multiple_of(jnp.maximum(first + STRETCH - WINDOW, 0), STRETCH)
        window = pl.ds(base, WINDOW)
        mine = pl.ds(pl.multiple_of(place * LANES, LANES), LANES)

        s = dot_nn(k_seq[window, :], q_t_ref[place])
        tops = [jnp.full((8, 128), -jnp.inf, F32) for _ in tiles]
        for r in steps:
            key = down + (base + r)
            allowed = (key >= low) & (key <= token)
            for j, cols in enumerate(tiles):
                x = jnp.where(allowed, s[r : r + SUB, cols], -jnp.inf)
                e_buf[r : r + SUB, cols] = x
                tops[j] = jnp.maximum(tops[j], folded(x, jnp.max))
        tops = [jnp.max(t, axis=0, keepdims=True) * factor for t in tops]

        dp = dot_nn(v_seq[window, :], do_t_ref[place])
        totals = [jnp.zeros((8, 128), F32) for _ in tiles]
        deltas = [jnp.zeros((8, 128), F32) for _ in tiles]
        for r in steps:
            for j, cols in enumerate(tiles):
                e = jnp.exp2(e_buf[r : r + SUB, cols] * factor - tops[j])
                d = dp[r : r + SUB, cols]
                e_buf[r : r + SUB, cols] = e
                dp_buf[r : r + SUB, cols] = d
                totals[j] = totals[j] + folded(e, jnp.sum)
                deltas[j] = deltas[j] + folded(e * d, jnp.sum)
        inverse = [1.0 / jnp.sum(t, axis=0, keepdims=True) for t in totals]
        deltas = [jnp.sum(d, axis=0, keepdims=True) * i for d, i in zip(deltas, inverse)]

        p_cols, ds_cols = [], []
        for j, cols in enumerate(tiles):
            p_rows, ds_rows = [], []
            for r in steps:
                p = e_buf[r : r + SUB, cols] * inverse[j]
                p_rows.append(p.astype(BF16))
                ds_rows.append((p * (dp_buf[r : r + SUB, cols] - deltas[j])).astype(BF16))
            p_cols.append(jnp.concatenate(p_rows, axis=0))
            ds_cols.append(jnp.concatenate(ds_rows, axis=0))
        p = jnp.concatenate(p_cols, axis=1)
        ds = jnp.concatenate(ds_cols, axis=1)
        dv_acc[window, :] += dot_nn(p, do_ref[mine, :])
        dk_acc[window, :] += dot_nn(ds, q_ref[mine, :])
        out = dot_tn(v_seq[window, :], p).T
        dq = dot_tn(k_seq[window, :], ds).T * SCALE
        rows = pl.ds(pl.multiple_of(place * STRETCH, STRETCH), STRETCH)
        cosine, signed_sine = expanded(mine_ref[rows, :])
        for head in range(HQ):
            cols = slice(head * HD, (head + 1) * HD)
            part = slice(head * STRETCH, (head + 1) * STRETCH)
            out_buf[rows, cols] = out[part].astype(BF16)
            dq_buf[rows, cols] = rotated_back(dq[part], cosine, signed_sine).astype(BF16)
        for copy in results(place):
            copy.start()
        return carry

    def results(place):
        rows = pl.ds(pl.multiple_of(place * STRETCH, STRETCH), STRETCH)
        return (
            pltpu.make_async_copy(out_buf.at[rows], out_ref.at[rows], sems.at[0, place]),
            pltpu.make_async_copy(dq_buf.at[rows], dq_ref.at[rows], sems.at[1, place]),
        )

    lax.fori_loop(0, 2, one_stretch, 0)
    for block in range(blocks):
        at = pl.ds(pl.multiple_of(order_ref[block] * STRETCH, STRETCH), STRETCH)
        rows = pl.ds((block % 2) * STRETCH, STRETCH)
        part_ref[block // 2, rows, :HD] = (dk_acc[at, :] * SCALE).astype(BF16)
        part_ref[block // 2, rows, HD:] = dv_acc[at, :].astype(BF16)
    for place in range(2):
        for copy in results(place):
            copy.wait()


def sums_kernel(parts_ref, mine_ref, dk_ref, dv_ref):
    total = parts_ref[0].astype(F32)
    for peer in range(1, parts_ref.shape[0]):
        total = total + parts_ref[peer].astype(F32)
    dk_ref[...] = rotated_back(total[:, :HD], *expanded(mine_ref[...])).astype(BF16)
    dv_ref[...] = total[:, HD:].astype(BF16)


def params(mib):
    return pltpu.CompilerParams(vmem_limit_bytes=mib * 2**20)


VMEM = pl.BlockSpec(memory_space=pltpu.VMEM)
HBM = pl.BlockSpec(memory_space=pltpu.HBM)
SMEM = pl.BlockSpec(memory_space=pltpu.SMEM)


def shards(queries, keys, values, out_grad, positions, doc_ids, stretch_order):
    devices = lax.axis_size("cp")
    rows = queries.shape[0]
    total = rows * devices
    shape = jax.ShapeDtypeStruct
    both = jnp.concatenate([keys, values], axis=1)
    payload = jnp.broadcast_to(both, (devices, *both.shape))
    kv = lax.all_to_all(payload, "cp", 0, 0, tiled=True)
    table, mine, q_rows, do_rows, q_cols, do_cols, starts = pl.pallas_call(
        tables_kernel,
        out_shape=(
            shape((total, HD), F32),
            shape((rows, HD), F32),
            shape((2 * LANES, HD), BF16),
            shape((2 * LANES, HD), BF16),
            shape((2, HD, LANES), BF16),
            shape((2, HD, LANES), BF16),
            shape((DOCS,), jnp.int32),
        ),
        in_specs=[SMEM, VMEM, VMEM, VMEM, VMEM],
        out_specs=(VMEM,) * 6 + (SMEM,),
        compiler_params=params(16),
        name="tables",
        cost_estimate=pl.CostEstimate(flops=10**7, transcendentals=0, bytes_accessed=4 * 10**6),
    )(stretch_order, positions, doc_ids.reshape(total // 128, 128), queries, out_grad)
    part, attn_out, grad_queries = pl.pallas_call(
        attention_kernel,
        out_shape=(
            shape((devices, rows, 2 * HD), BF16),
            shape((rows, HQ * HD), BF16),
            shape((rows, HQ * HD), BF16),
        ),
        in_specs=[SMEM, SMEM] + [VMEM] * 7,
        out_specs=(VMEM, HBM, HBM),
        scratch_shapes=[
            pltpu.VMEM((total, HD), BF16),
            pltpu.VMEM((total, HD), BF16),
            pltpu.VMEM((WINDOW, LANES), F32),
            pltpu.VMEM((WINDOW, LANES), F32),
            pltpu.VMEM((total, HD), F32),
            pltpu.VMEM((total, HD), F32),
            pltpu.VMEM((rows, HQ * HD), BF16),
            pltpu.VMEM((rows, HQ * HD), BF16),
            pltpu.SemaphoreType.DMA((2, 2)),
        ],
        compiler_params=params(24),
        name="attention",
    )(starts, stretch_order, kv, table, mine, q_rows, do_rows, q_cols, do_cols)
    parts = lax.all_to_all(part, "cp", 0, 0, tiled=True)
    grad_keys, grad_values = pl.pallas_call(
        sums_kernel,
        out_shape=(shape((rows, HD), BF16), shape((rows, HD), BF16)),
        in_specs=[VMEM] * 2,
        out_specs=(VMEM, VMEM),
        compiler_params=params(16),
        name="sums",
    )(parts, mine)
    return attn_out, grad_queries, grad_keys, grad_values


def solution(mesh):
    split = P(("seq", "cp"), None)
    return jax.shard_map(
        shards,
        mesh=mesh,
        in_specs=(split, split, split, split, P(None, "seq"), P("seq"), P("seq")),
        out_specs=(split, split, split, split),
        check_vma=False,
    )
```

```python
import math

import jax
import jax.numpy as jnp
from jax import lax
from jax.experimental import pallas as pl
from jax.experimental.pallas import tpu as pltpu
from jax.sharding import PartitionSpec as P

HQ = 6
HD = 128
HALF = HD // 2
SEC_T = 16
SEC_H = 24
STRETCH = 64
DOCS = 8
WINDOW = 1024 + STRETCH
SUB = 32
LANES = HQ * STRETCH
SCALE = 1.0 / math.sqrt(HD)
LOG2E = math.log2(math.e)

F32 = jnp.float32
BF16 = jnp.bfloat16


def dot_nt(left, right):
    return lax.dot_general(left, right, (((1,), (1,)), ((), ())), preferred_element_type=F32)


def dot_tn(left, right):
    return lax.dot_general(left, right, (((0,), (0,)), ((), ())), preferred_element_type=F32)


def dot_nn(left, right):
    return lax.dot_general(left, right, (((1,), (0,)), ((), ())), preferred_element_type=F32)


def rotated(x, cosine, signed_sine):
    return x * cosine + pltpu.roll(x, HALF, 1) * signed_sine


def rotated_back(x, cosine, signed_sine):
    return x * cosine - pltpu.roll(x, HALF, 1) * signed_sine


def prepare_kernel(
    order_ref, keys_ref, values_ref, pos_ref, docs_ref, queries_ref, grad_ref,
    payload_ref, cos_ref, sin_ref, q_ref, do_ref, q_t_ref, do_t_ref, starts_ref,
):
    me = lax.axis_index("cp")
    rows = keys_ref.shape[0]
    lane = lax.broadcasted_iota(jnp.int32, (1, rows), 1)
    windows = []
    for place in range(2):
        stretch = order_ref[2 * me + place]
        start = pl.multiple_of((stretch // 2) * 128, 128)
        window = pos_ref[:, pl.ds(start, 128)].astype(F32)
        turned = pltpu.roll(window, HALF, 1)
        windows.append(jnp.where(stretch % 2 == place, window, turned))
    pos = jnp.where(lane < STRETCH, windows[0], windows[1])
    pair = lax.broadcasted_iota(jnp.int32, (HALF, 1), 0)
    freq = jnp.exp(-(2.0 * pair.astype(F32) / HD) * math.log(1000000.0))
    chosen = jnp.where(
        pair < SEC_T, pos[0:1, :], jnp.where(pair < SEC_T + SEC_H, pos[1:2, :], pos[2:3, :])
    )
    angle = chosen * freq
    table = jnp.concatenate([jnp.cos(angle), jnp.sin(angle)], axis=0).T
    other = pltpu.roll(table, HALF, 1)
    column = lax.broadcasted_iota(jnp.int32, (1, HD), 1)
    cosine = jnp.where(column < HALF, table, other)
    signed_sine = jnp.where(column < HALF, -other, table)
    cos_ref[...] = cosine
    sin_ref[...] = signed_sine
    k_rot = rotated(keys_ref[...].astype(F32), cosine, signed_sine).astype(BF16)
    values = values_ref[...]
    for peer in range(payload_ref.shape[0]):
        payload_ref[peer, :, :HD] = k_rot
        payload_ref[peer, :, HD:] = values
    for place in range(2):
        part = slice(place * STRETCH, (place + 1) * STRETCH)
        for head in range(HQ):
            cols = slice(head * HD, (head + 1) * HD)
            to = pl.ds(place * LANES + head * STRETCH, STRETCH)
            q_ref[to, :] = rotated(
                queries_ref[part, cols].astype(F32), cosine[part], signed_sine[part]
            ).astype(BF16)
            do_ref[to, :] = grad_ref[part, cols]
        half = pl.ds(place * LANES, LANES)
        q_t_ref[place] = q_ref[half, :].T
        do_t_ref[place] = do_ref[half, :].T
    docs = docs_ref[...]
    for doc in range(DOCS):
        starts_ref[doc] = jnp.sum((docs < doc).astype(jnp.int32))


def attention_kernel(
    starts_ref, order_ref, kv_ref, cos_ref, sin_ref, q_ref, do_ref, q_t_ref, do_t_ref,
    part_ref, out_ref, dq_ref,
    k_seq, v_seq, e_buf, dp_buf, dk_acc, dv_acc, out_buf, dq_buf, sems,
):
    me = lax.axis_index("cp")
    blocks = k_seq.shape[0] // STRETCH
    for block in range(blocks):
        to = pl.ds(pl.multiple_of(order_ref[block] * STRETCH, STRETCH), STRETCH)
        rows = pl.ds((block % 2) * STRETCH, STRETCH)
        k_seq[to, :] = kv_ref[block // 2, rows, :HD]
        v_seq[to, :] = kv_ref[block // 2, rows, HD:]
    dk_acc[...] = jnp.zeros_like(dk_acc)
    dv_acc[...] = jnp.zeros_like(dv_acc)
    tiles = [slice(j * 128, (j + 1) * 128) for j in range(LANES // 128)]
    steps = range(0, WINDOW, SUB)
    lane = lax.broadcasted_iota(jnp.int32, (1, 128), 1)
    down = lax.broadcasted_iota(jnp.int32, (SUB, 128), 0)
    factor = SCALE * LOG2E

    def folded(x, how):
        return how(x.reshape(SUB // 8, 8, 128), axis=0)

    def one_stretch(place, carry):
        first = order_ref[2 * me + place] * STRETCH
        token = first + lane % STRETCH
        low = jnp.zeros_like(token)
        for doc in range(DOCS):
            start = starts_ref[doc]
            low = jnp.where(start <= token, jnp.maximum(low, start), low)
        base = pl.multiple_of(jnp.maximum(first + STRETCH - WINDOW, 0), STRETCH)
        window = pl.ds(base, WINDOW)
        mine = pl.ds(pl.multiple_of(place * LANES, LANES), LANES)

        s = dot_nn(k_seq[window, :], q_t_ref[place])
        tops = [jnp.full((8, 128), -jnp.inf, F32) for _ in tiles]
        for r in steps:
            key = down + (base + r)
            allowed = (key >= low) & (key <= token)
            for j, cols in enumerate(tiles):
                x = jnp.where(allowed, s[r : r + SUB, cols], -jnp.inf)
                e_buf[r : r + SUB, cols] = x
                tops[j] = jnp.maximum(tops[j], folded(x, jnp.max))
        tops = [jnp.max(t, axis=0, keepdims=True) * factor for t in tops]

        dp = dot_nn(v_seq[window, :], do_t_ref[place])
        totals = [jnp.zeros((8, 128), F32) for _ in tiles]
        deltas = [jnp.zeros((8, 128), F32) for _ in tiles]
        for r in steps:
            for j, cols in enumerate(tiles):
                e = jnp.exp2(e_buf[r : r + SUB, cols] * factor - tops[j])
                d = dp[r : r + SUB, cols]
                e_buf[r : r + SUB, cols] = e
                dp_buf[r : r + SUB, cols] = d
                totals[j] = totals[j] + folded(e, jnp.sum)
                deltas[j] = deltas[j] + folded(e * d, jnp.sum)
        inverse = [1.0 / jnp.sum(t, axis=0, keepdims=True) for t in totals]
        deltas = [jnp.sum(d, axis=0, keepdims=True) * i for d, i in zip(deltas, inverse)]

        p_cols, ds_cols = [], []
        for j, cols in enumerate(tiles):
            p_rows, ds_rows = [], []
            for r in steps:
                p = e_buf[r : r + SUB, cols] * inverse[j]
                p_rows.append(p.astype(BF16))
                ds_rows.append((p * (dp_buf[r : r + SUB, cols] - deltas[j])).astype(BF16))
            p_cols.append(jnp.concatenate(p_rows, axis=0))
            ds_cols.append(jnp.concatenate(ds_rows, axis=0))
        p = jnp.concatenate(p_cols, axis=1)
        ds = jnp.concatenate(ds_cols, axis=1)
        out = dot_tn(v_seq[window, :], p).T
        dq = dot_tn(k_seq[window, :], ds).T * SCALE
        rows = pl.ds(pl.multiple_of(place * STRETCH, STRETCH), STRETCH)
        cosine, signed_sine = cos_ref[rows, :], sin_ref[rows, :]
        for head in range(HQ):
            cols = slice(head * HD, (head + 1) * HD)
            part = slice(head * STRETCH, (head + 1) * STRETCH)
            out_buf[rows, cols] = out[part].astype(BF16)
            dq_buf[rows, cols] = rotated_back(dq[part], cosine, signed_sine).astype(BF16)
        for copy in results(place):
            copy.start()
        dv_acc[window, :] += dot_nn(p, do_ref[mine, :])
        dk_acc[window, :] += dot_nn(ds, q_ref[mine, :])
        return carry

    def results(place):
        rows = pl.ds(pl.multiple_of(place * STRETCH, STRETCH), STRETCH)
        return (
            pltpu.make_async_copy(out_buf.at[rows], out_ref.at[rows], sems.at[0, place]),
            pltpu.make_async_copy(dq_buf.at[rows], dq_ref.at[rows], sems.at[1, place]),
        )

    lax.fori_loop(0, 2, one_stretch, 0)
    for block in range(blocks):
        at = pl.ds(pl.multiple_of(order_ref[block] * STRETCH, STRETCH), STRETCH)
        rows = pl.ds((block % 2) * STRETCH, STRETCH)
        part_ref[block // 2, rows, :HD] = (dk_acc[at, :] * SCALE).astype(BF16)
        part_ref[block // 2, rows, HD:] = dv_acc[at, :].astype(BF16)
    for place in range(2):
        for copy in results(place):
            copy.wait()


def sums_kernel(parts_ref, cos_ref, sin_ref, dk_ref, dv_ref):
    total = parts_ref[0].astype(F32)
    for peer in range(1, parts_ref.shape[0]):
        total = total + parts_ref[peer].astype(F32)
    dk_ref[...] = rotated_back(total[:, :HD], cos_ref[...], sin_ref[...]).astype(BF16)
    dv_ref[...] = total[:, HD:].astype(BF16)


def in_hbm(x):
    return pltpu.with_memory_space_constraint(x, pltpu.HBM)


def params(mib):
    return pltpu.CompilerParams(vmem_limit_bytes=mib * 2**20)


VMEM = pl.BlockSpec(memory_space=pltpu.VMEM)
HBM = pl.BlockSpec(memory_space=pltpu.HBM)
SMEM = pl.BlockSpec(memory_space=pltpu.SMEM)


def shards(queries, keys, values, out_grad, positions, doc_ids, stretch_order):
    devices = lax.axis_size("cp")
    rows = queries.shape[0]
    total = rows * devices
    shape = jax.ShapeDtypeStruct
    stretch_order = in_hbm(stretch_order)
    docs = doc_ids.reshape(total // 128, 128)
    payload, cosine, sine, q_rows, do_rows, q_cols, do_cols, starts = pl.pallas_call(
        prepare_kernel,
        out_shape=(
            shape((devices, rows, 2 * HD), BF16),
            shape((rows, HD), F32),
            shape((rows, HD), F32),
            shape((2 * LANES, HD), BF16),
            shape((2 * LANES, HD), BF16),
            shape((2, HD, LANES), BF16),
            shape((2, HD, LANES), BF16),
            shape((DOCS,), jnp.int32),
        ),
        in_specs=[SMEM] + [VMEM] * 6,
        out_specs=(VMEM,) * 7 + (SMEM,),
        compiler_params=params(16),
        name="prepare",
    )(
        stretch_order,
        *(in_hbm(x) for x in (keys, values, positions, docs, queries, out_grad)),
    )
    kv = lax.all_to_all(payload, "cp", 0, 0, tiled=True)
    part, attn_out, grad_queries = pl.pallas_call(
        attention_kernel,
        out_shape=(
            shape((devices, rows, 2 * HD), BF16),
            shape((rows, HQ * HD), BF16),
            shape((rows, HQ * HD), BF16),
        ),
        in_specs=[SMEM, SMEM] + [VMEM] * 7,
        out_specs=(VMEM, HBM, HBM),
        scratch_shapes=[
            pltpu.VMEM((total, HD), BF16),
            pltpu.VMEM((total, HD), BF16),
            pltpu.VMEM((WINDOW, LANES), F32),
            pltpu.VMEM((WINDOW, LANES), F32),
            pltpu.VMEM((total, HD), F32),
            pltpu.VMEM((total, HD), F32),
            pltpu.VMEM((rows, HQ * HD), BF16),
            pltpu.VMEM((rows, HQ * HD), BF16),
            pltpu.SemaphoreType.DMA((2, 2)),
        ],
        compiler_params=params(24),
        name="attention",
    )(starts, stretch_order, kv, cosine, sine, q_rows, do_rows, q_cols, do_cols)
    parts = lax.all_to_all(part, "cp", 0, 0, tiled=True)
    grad_keys, grad_values = pl.pallas_call(
        sums_kernel,
        out_shape=(shape((rows, HD), BF16), shape((rows, HD), BF16)),
        in_specs=[VMEM] * 3,
        out_specs=(VMEM, VMEM),
        compiler_params=params(16),
        name="sums",
    )(parts, cosine, sine)
    return attn_out, grad_queries, grad_keys, grad_values


def solution(mesh):
    split = P(("seq", "cp"), None)
    return jax.shard_map(
        shards,
        mesh=mesh,
        in_specs=(split, split, split, split, P(None, "seq"), P("seq"), P("seq")),
        out_specs=(split, split, split, split),
        check_vma=False,
    )
```

```python
import math

import jax
import jax.numpy as jnp
from jax import lax
from jax.experimental import pallas as pl
from jax.experimental.pallas import tpu as pltpu
from jax.sharding import PartitionSpec as P

HQ = 6
HD = 128
HALF = HD // 2
SEC_T = 16
SEC_H = 24
STRETCH = 64
DOCS = 8
WINDOW = 1024 + STRETCH
SUB = 32
LANES = HQ * STRETCH
SCALE = 1.0 / math.sqrt(HD)
LOG2E = math.log2(math.e)

F32 = jnp.float32
BF16 = jnp.bfloat16


def dot_nt(left, right):
    return lax.dot_general(left, right, (((1,), (1,)), ((), ())), preferred_element_type=F32)


def dot_tn(left, right):
    return lax.dot_general(left, right, (((0,), (0,)), ((), ())), preferred_element_type=F32)


def dot_nn(left, right):
    return lax.dot_general(left, right, (((1,), (0,)), ((), ())), preferred_element_type=F32)


def rotated(x, cosine, signed_sine):
    return x * cosine + pltpu.roll(x, HALF, 1) * signed_sine


def rotated_back(x, cosine, signed_sine):
    return x * cosine - pltpu.roll(x, HALF, 1) * signed_sine


def prepare_kernel(
    order_ref, keys_ref, values_ref, pos_ref, docs_ref, queries_ref, grad_ref,
    payload_ref, cos_ref, sin_ref, q_ref, do_ref, q_t_ref, do_t_ref, facts_ref,
):
    me = lax.axis_index("cp")
    rows = keys_ref.shape[0]
    lane = lax.broadcasted_iota(jnp.int32, (1, rows), 1)
    windows = []
    for place in range(2):
        stretch = order_ref[2 * me + place]
        start = pl.multiple_of((stretch // 2) * 128, 128)
        window = pos_ref[:, pl.ds(start, 128)].astype(F32)
        turned = pltpu.roll(window, HALF, 1)
        windows.append(jnp.where(stretch % 2 == place, window, turned))
    pos = jnp.where(lane < STRETCH, windows[0], windows[1])
    pair = lax.broadcasted_iota(jnp.int32, (HALF, 1), 0)
    freq = jnp.exp(-(2.0 * pair.astype(F32) / HD) * math.log(1000000.0))
    chosen = jnp.where(
        pair < SEC_T, pos[0:1, :], jnp.where(pair < SEC_T + SEC_H, pos[1:2, :], pos[2:3, :])
    )
    angle = chosen * freq
    table = jnp.concatenate([jnp.cos(angle), jnp.sin(angle)], axis=0).T
    other = pltpu.roll(table, HALF, 1)
    column = lax.broadcasted_iota(jnp.int32, (1, HD), 1)
    cosine = jnp.where(column < HALF, table, other)
    signed_sine = jnp.where(column < HALF, -other, table)
    cos_ref[...] = cosine
    sin_ref[...] = signed_sine
    k_rot = rotated(keys_ref[...].astype(F32), cosine, signed_sine).astype(BF16)
    values = values_ref[...]
    for peer in range(payload_ref.shape[0]):
        payload_ref[peer, :, :HD] = k_rot
        payload_ref[peer, :, HD:] = values
    for place in range(2):
        part = slice(place * STRETCH, (place + 1) * STRETCH)
        for head in range(HQ):
            cols = slice(head * HD, (head + 1) * HD)
            to = pl.ds(place * LANES + head * STRETCH, STRETCH)
            q_ref[to, :] = rotated(
                queries_ref[part, cols].astype(F32), cosine[part], signed_sine[part]
            ).astype(BF16)
            do_ref[to, :] = grad_ref[part, cols]
        half = pl.ds(place * LANES, LANES)
        q_t_ref[place] = q_ref[half, :].T
        do_t_ref[place] = do_ref[half, :].T
    docs = docs_ref[...]
    starts = [jnp.sum((docs < doc).astype(jnp.int32)) for doc in range(DOCS)]
    lanes = lax.broadcasted_iota(jnp.int32, (1, 128), 1)
    order = jnp.zeros((1, 128), jnp.int32)
    for block in range(order_ref.shape[0]):
        order = jnp.where(lanes == block, order_ref[block], order)
    firsts = [order_ref[2 * me + place] * STRETCH for place in range(2)]
    facts_ref[0:1, :] = order
    facts_ref[1:2, :] = jnp.where(lanes == 0, firsts[0], firsts[1])
    for place, first in enumerate(firsts):
        token = first + lanes % STRETCH
        low = jnp.zeros((1, 128), jnp.int32)
        for start in starts:
            low = jnp.where(start <= token, jnp.maximum(low, start), low)
        facts_ref[2 + place : 3 + place, :] = low
        facts_ref[4 + place : 5 + place, :] = token


def attention_kernel(
    facts_ref, kv_ref, cos_ref, sin_ref, q_ref, do_ref, q_t_ref, do_t_ref,
    part_ref, out_ref, dq_ref,
    k_seq, v_seq, e_buf, dp_buf, dk_acc, dv_acc, out_buf, dq_buf, sems,
):
    blocks = k_seq.shape[0] // STRETCH
    for block in range(blocks):
        to = pl.ds(pl.multiple_of(facts_ref[0, block] * STRETCH, STRETCH), STRETCH)
        rows = pl.ds((block % 2) * STRETCH, STRETCH)
        k_seq[to, :] = kv_ref[block // 2, rows, :HD]
        v_seq[to, :] = kv_ref[block // 2, rows, HD:]
    dk_acc[...] = jnp.zeros_like(dk_acc)
    dv_acc[...] = jnp.zeros_like(dv_acc)
    tiles = [slice(j * 128, (j + 1) * 128) for j in range(LANES // 128)]
    steps = range(0, WINDOW, SUB)
    down = lax.broadcasted_iota(jnp.int32, (SUB, 128), 0)
    factor = SCALE * LOG2E

    def folded(x, how):
        return how(x.reshape(SUB // 8, 8, 128), axis=0)

    def one_stretch(place, carry):
        first = jnp.where(place == 0, facts_ref[1, 0], facts_ref[1, 1])
        low = facts_ref[pl.ds(2 + place, 1), :]
        token = facts_ref[pl.ds(4 + place, 1), :]
        base = pl.multiple_of(jnp.maximum(first + STRETCH - WINDOW, 0), STRETCH)
        window = pl.ds(base, WINDOW)
        mine = pl.ds(pl.multiple_of(place * LANES, LANES), LANES)

        s = dot_nn(k_seq[window, :], q_t_ref[place])
        tops = [jnp.full((8, 128), -jnp.inf, F32) for _ in tiles]
        for r in steps:
            key = down + (base + r)
            allowed = (key >= low) & (key <= token)
            for j, cols in enumerate(tiles):
                x = jnp.where(allowed, s[r : r + SUB, cols], -jnp.inf)
                e_buf[r : r + SUB, cols] = x
                tops[j] = jnp.maximum(tops[j], folded(x, jnp.max))
        tops = [jnp.max(t, axis=0, keepdims=True) * factor for t in tops]

        dp = dot_nn(v_seq[window, :], do_t_ref[place])
        totals = [jnp.zeros((8, 128), F32) for _ in tiles]
        deltas = [jnp.zeros((8, 128), F32) for _ in tiles]
        for r in steps:
            for j, cols in enumerate(tiles):
                e = jnp.exp2(e_buf[r : r + SUB, cols] * factor - tops[j])
                d = dp[r : r + SUB, cols]
                e_buf[r : r + SUB, cols] = e
                dp_buf[r : r + SUB, cols] = d
                totals[j] = totals[j] + folded(e, jnp.sum)
                deltas[j] = deltas[j] + folded(e * d, jnp.sum)
        inverse = [1.0 / jnp.sum(t, axis=0, keepdims=True) for t in totals]
        deltas = [jnp.sum(d, axis=0, keepdims=True) * i for d, i in zip(deltas, inverse)]

        p_cols, ds_cols = [], []
        for j, cols in enumerate(tiles):
            p_rows, ds_rows = [], []
            for r in steps:
                p = e_buf[r : r + SUB, cols] * inverse[j]
                p_rows.append(p.astype(BF16))
                ds_rows.append((p * (dp_buf[r : r + SUB, cols] - deltas[j])).astype(BF16))
            p_cols.append(jnp.concatenate(p_rows, axis=0))
            ds_cols.append(jnp.concatenate(ds_rows, axis=0))
        p = jnp.concatenate(p_cols, axis=1)
        ds = jnp.concatenate(ds_cols, axis=1)
        out = dot_tn(v_seq[window, :], p).T
        dq = dot_tn(k_seq[window, :], ds).T * SCALE
        rows = pl.ds(pl.multiple_of(place * STRETCH, STRETCH), STRETCH)
        cosine, signed_sine = cos_ref[rows, :], sin_ref[rows, :]
        for head in range(HQ):
            cols = slice(head * HD, (head + 1) * HD)
            part = slice(head * STRETCH, (head + 1) * STRETCH)
            out_buf[rows, cols] = out[part].astype(BF16)
            dq_buf[rows, cols] = rotated_back(dq[part], cosine, signed_sine).astype(BF16)
        for copy in results(place):
            copy.start()
        dv_acc[window, :] += dot_nn(p, do_ref[mine, :])
        dk_acc[window, :] += dot_nn(ds, q_ref[mine, :])
        return carry

    def results(place):
        rows = pl.ds(pl.multiple_of(place * STRETCH, STRETCH), STRETCH)
        return (
            pltpu.make_async_copy(out_buf.at[rows], out_ref.at[rows], sems.at[0, place]),
            pltpu.make_async_copy(dq_buf.at[rows], dq_ref.at[rows], sems.at[1, place]),
        )

    lax.fori_loop(0, 2, one_stretch, 0)
    for block in range(blocks):
        at = pl.ds(pl.multiple_of(facts_ref[0, block] * STRETCH, STRETCH), STRETCH)
        rows = pl.ds((block % 2) * STRETCH, STRETCH)
        part_ref[block // 2, rows, :HD] = (dk_acc[at, :] * SCALE).astype(BF16)
        part_ref[block // 2, rows, HD:] = dv_acc[at, :].astype(BF16)
    for place in range(2):
        for copy in results(place):
            copy.wait()


def sums_kernel(parts_ref, cos_ref, sin_ref, dk_ref, dv_ref):
    total = parts_ref[0].astype(F32)
    for peer in range(1, parts_ref.shape[0]):
        total = total + parts_ref[peer].astype(F32)
    dk_ref[...] = rotated_back(total[:, :HD], cos_ref[...], sin_ref[...]).astype(BF16)
    dv_ref[...] = total[:, HD:].astype(BF16)


def in_hbm(x):
    return pltpu.with_memory_space_constraint(x, pltpu.HBM)


def params(mib):
    return pltpu.CompilerParams(vmem_limit_bytes=mib * 2**20)


VMEM = pl.BlockSpec(memory_space=pltpu.VMEM)
HBM = pl.BlockSpec(memory_space=pltpu.HBM)
SMEM = pl.BlockSpec(memory_space=pltpu.SMEM)


def shards(queries, keys, values, out_grad, positions, doc_ids, stretch_order):
    devices = lax.axis_size("cp")
    rows = queries.shape[0]
    total = rows * devices
    shape = jax.ShapeDtypeStruct
    docs = doc_ids.reshape(total // 128, 128)
    payload, cosine, sine, q_rows, do_rows, q_cols, do_cols, facts = pl.pallas_call(
        prepare_kernel,
        out_shape=(
            shape((devices, rows, 2 * HD), BF16),
            shape((rows, HD), F32),
            shape((rows, HD), F32),
            shape((2 * LANES, HD), BF16),
            shape((2 * LANES, HD), BF16),
            shape((2, HD, LANES), BF16),
            shape((2, HD, LANES), BF16),
            shape((8, 128), jnp.int32),
        ),
        in_specs=[SMEM] + [VMEM] * 6,
        out_specs=(VMEM,) * 8,
        compiler_params=params(16),
        name="prepare",
    )(
        *(in_hbm(x) for x in (stretch_order, keys, values, positions, docs, queries, out_grad)),
    )
    kv = lax.all_to_all(payload, "cp", 0, 0, tiled=True)
    part, attn_out, grad_queries = pl.pallas_call(
        attention_kernel,
        out_shape=(
            shape((devices, rows, 2 * HD), BF16),
            shape((rows, HQ * HD), BF16),
            shape((rows, HQ * HD), BF16),
        ),
        in_specs=[VMEM] * 8,
        out_specs=(VMEM, HBM, HBM),
        scratch_shapes=[
            pltpu.VMEM((total, HD), BF16),
            pltpu.VMEM((total, HD), BF16),
            pltpu.VMEM((WINDOW, LANES), F32),
            pltpu.VMEM((WINDOW, LANES), F32),
            pltpu.VMEM((total, HD), F32),
            pltpu.VMEM((total, HD), F32),
            pltpu.VMEM((rows, HQ * HD), BF16),
            pltpu.VMEM((rows, HQ * HD), BF16),
            pltpu.SemaphoreType.DMA((2, 2)),
        ],
        compiler_params=params(24),
        name="attention",
    )(facts, kv, cosine, sine, q_rows, do_rows, q_cols, do_cols)
    parts = lax.all_to_all(part, "cp", 0, 0, tiled=True)
    grad_keys, grad_values = pl.pallas_call(
        sums_kernel,
        out_shape=(shape((rows, HD), BF16), shape((rows, HD), BF16)),
        in_specs=[VMEM] * 3,
        out_specs=(VMEM, VMEM),
        compiler_params=params(16),
        name="sums",
    )(parts, cosine, sine)
    return attn_out, grad_queries, grad_keys, grad_values


def solution(mesh):
    split = P(("seq", "cp"), None)
    return jax.shard_map(
        shards,
        mesh=mesh,
        in_specs=(split, split, split, split, P(None, "seq"), P("seq"), P("seq")),
        out_specs=(split, split, split, split),
        check_vma=False,
    )
```

```python
import math

import jax
import jax.numpy as jnp
from jax import lax
from jax.experimental import pallas as pl
from jax.experimental.pallas import tpu as pltpu
from jax.sharding import PartitionSpec as P

HQ = 6
HD = 128
HALF = HD // 2
SEC_T = 16
SEC_H = 24
STRETCH = 64
DOCS = 8
WINDOW = 1024 + STRETCH
SUB = 32
LANES = HQ * STRETCH
SCALE = 1.0 / math.sqrt(HD)
LOG2E = math.log2(math.e)

F32 = jnp.float32
BF16 = jnp.bfloat16


def dot_nt(left, right):
    return lax.dot_general(left, right, (((1,), (1,)), ((), ())), preferred_element_type=F32)


def dot_tn(left, right):
    return lax.dot_general(left, right, (((0,), (0,)), ((), ())), preferred_element_type=F32)


def dot_nn(left, right):
    return lax.dot_general(left, right, (((1,), (0,)), ((), ())), preferred_element_type=F32)


def rotated(x, cosine, signed_sine):
    return x * cosine + pltpu.roll(x, HALF, 1) * signed_sine


def rotated_back(x, cosine, signed_sine):
    return x * cosine - pltpu.roll(x, HALF, 1) * signed_sine


def prepare_kernel(
    order_ref, keys_ref, values_ref, pos_ref, docs_ref, payload_ref, cos_ref, sin_ref, facts_ref
):
    me = lax.axis_index("cp")
    rows = keys_ref.shape[0]
    lane = lax.broadcasted_iota(jnp.int32, (1, rows), 1)
    windows = []
    for place in range(2):
        stretch = order_ref[2 * me + place]
        start = pl.multiple_of((stretch // 2) * 128, 128)
        window = pos_ref[:, pl.ds(start, 128)].astype(F32)
        turned = pltpu.roll(window, HALF, 1)
        windows.append(jnp.where(stretch % 2 == place, window, turned))
    pos = jnp.where(lane < STRETCH, windows[0], windows[1])
    pair = lax.broadcasted_iota(jnp.int32, (HALF, 1), 0)
    freq = jnp.exp(-(2.0 * pair.astype(F32) / HD) * math.log(1000000.0))
    chosen = jnp.where(
        pair < SEC_T, pos[0:1, :], jnp.where(pair < SEC_T + SEC_H, pos[1:2, :], pos[2:3, :])
    )
    angle = chosen * freq
    table = jnp.concatenate([jnp.cos(angle), jnp.sin(angle)], axis=0).T
    other = pltpu.roll(table, HALF, 1)
    column = lax.broadcasted_iota(jnp.int32, (1, HD), 1)
    cosine = jnp.where(column < HALF, table, other)
    signed_sine = jnp.where(column < HALF, -other, table)
    cos_ref[...] = cosine
    sin_ref[...] = signed_sine
    k_rot = rotated(keys_ref[...].astype(F32), cosine, signed_sine).astype(BF16)
    values = values_ref[...]
    for peer in range(payload_ref.shape[0]):
        payload_ref[peer, :, :HD] = k_rot
        payload_ref[peer, :, HD:] = values
    docs = docs_ref[...]
    starts = [jnp.sum((docs < doc).astype(jnp.int32)) for doc in range(DOCS)]
    lanes = lax.broadcasted_iota(jnp.int32, (1, 128), 1)
    order = jnp.zeros((1, 128), jnp.int32)
    for block in range(order_ref.shape[0]):
        order = jnp.where(lanes == block, order_ref[block], order)
    firsts = [order_ref[2 * me + place] * STRETCH for place in range(2)]
    facts_ref[0:1, :] = order
    facts_ref[1:2, :] = jnp.where(lanes == 0, firsts[0], firsts[1])
    for place, first in enumerate(firsts):
        token = first + lanes % STRETCH
        low = jnp.zeros((1, 128), jnp.int32)
        for start in starts:
            low = jnp.where(start <= token, jnp.maximum(low, start), low)
        facts_ref[2 + place : 3 + place, :] = low
        facts_ref[4 + place : 5 + place, :] = token


def attention_kernel(
    facts_ref, kv_ref, cos_ref, sin_ref, queries_ref, grad_ref,
    part_ref, out_ref, dq_ref,
    q_ref, do_ref, q_t_ref, do_t_ref, k_seq, v_seq, e_buf, dp_buf, dk_acc, dv_acc, out_buf, dq_buf, sems,
):
    cosine, signed_sine = cos_ref[...], sin_ref[...]
    for place in range(2):
        part = slice(place * STRETCH, (place + 1) * STRETCH)
        for head in range(HQ):
            cols = slice(head * HD, (head + 1) * HD)
            to = pl.ds(place * LANES + head * STRETCH, STRETCH)
            q_ref[to, :] = rotated(
                queries_ref[part, cols].astype(F32), cosine[part], signed_sine[part]
            ).astype(BF16)
            do_ref[to, :] = grad_ref[part, cols]
        half = pl.ds(place * LANES, LANES)
        q_t_ref[place] = q_ref[half, :].T
        do_t_ref[place] = do_ref[half, :].T
    blocks = k_seq.shape[0] // STRETCH
    for block in range(blocks):
        to = pl.ds(pl.multiple_of(facts_ref[0, block] * STRETCH, STRETCH), STRETCH)
        rows = pl.ds((block % 2) * STRETCH, STRETCH)
        k_seq[to, :] = kv_ref[block // 2, rows, :HD]
        v_seq[to, :] = kv_ref[block // 2, rows, HD:]
    dk_acc[...] = jnp.zeros_like(dk_acc)
    dv_acc[...] = jnp.zeros_like(dv_acc)
    tiles = [slice(j * 128, (j + 1) * 128) for j in range(LANES // 128)]
    steps = range(0, WINDOW, SUB)
    down = lax.broadcasted_iota(jnp.int32, (SUB, 128), 0)
    factor = SCALE * LOG2E

    def folded(x, how):
        return how(x.reshape(SUB // 8, 8, 128), axis=0)

    def one_stretch(place, carry):
        first = jnp.where(place == 0, facts_ref[1, 0], facts_ref[1, 1])
        low = facts_ref[pl.ds(2 + place, 1), :]
        token = facts_ref[pl.ds(4 + place, 1), :]
        base = pl.multiple_of(jnp.maximum(first + STRETCH - WINDOW, 0), STRETCH)
        window = pl.ds(base, WINDOW)
        mine = pl.ds(pl.multiple_of(place * LANES, LANES), LANES)

        s = dot_nn(k_seq[window, :], q_t_ref[place])
        tops = [jnp.full((8, 128), -jnp.inf, F32) for _ in tiles]
        for r in steps:
            key = down + (base + r)
            allowed = (key >= low) & (key <= token)
            for j, cols in enumerate(tiles):
                x = jnp.where(allowed, s[r : r + SUB, cols], -jnp.inf)
                e_buf[r : r + SUB, cols] = x
                tops[j] = jnp.maximum(tops[j], folded(x, jnp.max))
        tops = [jnp.max(t, axis=0, keepdims=True) * factor for t in tops]

        dp = dot_nn(v_seq[window, :], do_t_ref[place])
        totals = [jnp.zeros((8, 128), F32) for _ in tiles]
        deltas = [jnp.zeros((8, 128), F32) for _ in tiles]
        for r in steps:
            for j, cols in enumerate(tiles):
                e = jnp.exp2(e_buf[r : r + SUB, cols] * factor - tops[j])
                d = dp[r : r + SUB, cols]
                e_buf[r : r + SUB, cols] = e
                dp_buf[r : r + SUB, cols] = d
                totals[j] = totals[j] + folded(e, jnp.sum)
                deltas[j] = deltas[j] + folded(e * d, jnp.sum)
        inverse = [1.0 / jnp.sum(t, axis=0, keepdims=True) for t in totals]
        deltas = [jnp.sum(d, axis=0, keepdims=True) * i for d, i in zip(deltas, inverse)]

        p_cols, ds_cols = [], []
        for j, cols in enumerate(tiles):
            p_rows, ds_rows = [], []
            for r in steps:
                p = e_buf[r : r + SUB, cols] * inverse[j]
                p_rows.append(p.astype(BF16))
                ds_rows.append((p * (dp_buf[r : r + SUB, cols] - deltas[j])).astype(BF16))
            p_cols.append(jnp.concatenate(p_rows, axis=0))
            ds_cols.append(jnp.concatenate(ds_rows, axis=0))
        p = jnp.concatenate(p_cols, axis=1)
        ds = jnp.concatenate(ds_cols, axis=1)
        out = dot_tn(v_seq[window, :], p).T
        dq = dot_tn(k_seq[window, :], ds).T * SCALE
        rows = pl.ds(pl.multiple_of(place * STRETCH, STRETCH), STRETCH)
        cosine, signed_sine = cos_ref[rows, :], sin_ref[rows, :]
        for head in range(HQ):
            cols = slice(head * HD, (head + 1) * HD)
            part = slice(head * STRETCH, (head + 1) * STRETCH)
            out_buf[rows, cols] = out[part].astype(BF16)
            dq_buf[rows, cols] = rotated_back(dq[part], cosine, signed_sine).astype(BF16)
        for copy in results(place):
            copy.start()
        dv_acc[window, :] += dot_nn(p, do_ref[mine, :])
        dk_acc[window, :] += dot_nn(ds, q_ref[mine, :])
        return carry

    def results(place):
        rows = pl.ds(pl.multiple_of(place * STRETCH, STRETCH), STRETCH)
        return (
            pltpu.make_async_copy(out_buf.at[rows], out_ref.at[rows], sems.at[0, place]),
            pltpu.make_async_copy(dq_buf.at[rows], dq_ref.at[rows], sems.at[1, place]),
        )

    lax.fori_loop(0, 2, one_stretch, 0)
    for block in range(blocks):
        at = pl.ds(pl.multiple_of(facts_ref[0, block] * STRETCH, STRETCH), STRETCH)
        rows = pl.ds((block % 2) * STRETCH, STRETCH)
        part_ref[block // 2, rows, :HD] = (dk_acc[at, :] * SCALE).astype(BF16)
        part_ref[block // 2, rows, HD:] = dv_acc[at, :].astype(BF16)
    for place in range(2):
        for copy in results(place):
            copy.wait()


def sums_kernel(parts_ref, cos_ref, sin_ref, dk_ref, dv_ref):
    total = parts_ref[0].astype(F32)
    for peer in range(1, parts_ref.shape[0]):
        total = total + parts_ref[peer].astype(F32)
    dk_ref[...] = rotated_back(total[:, :HD], cos_ref[...], sin_ref[...]).astype(BF16)
    dv_ref[...] = total[:, HD:].astype(BF16)


def in_hbm(x):
    return pltpu.with_memory_space_constraint(x, pltpu.HBM)


def params(mib):
    return pltpu.CompilerParams(vmem_limit_bytes=mib * 2**20)


VMEM = pl.BlockSpec(memory_space=pltpu.VMEM)
HBM = pl.BlockSpec(memory_space=pltpu.HBM)
SMEM = pl.BlockSpec(memory_space=pltpu.SMEM)


def shards(queries, keys, values, out_grad, positions, doc_ids, stretch_order):
    devices = lax.axis_size("cp")
    rows = queries.shape[0]
    total = rows * devices
    shape = jax.ShapeDtypeStruct
    docs = doc_ids.reshape(total // 128, 128)
    payload, cosine, sine, facts = pl.pallas_call(
        prepare_kernel,
        out_shape=(
            shape((devices, rows, 2 * HD), BF16),
            shape((rows, HD), F32),
            shape((rows, HD), F32),
            shape((8, 128), jnp.int32),
        ),
        in_specs=[SMEM] + [VMEM] * 4,
        out_specs=(VMEM,) * 4,
        compiler_params=params(16),
        name="prepare",
    )(
        *(in_hbm(x) for x in (stretch_order, keys, values, positions, docs)),
    )
    kv = lax.all_to_all(payload, "cp", 0, 0, tiled=True)
    part, attn_out, grad_queries = pl.pallas_call(
        attention_kernel,
        out_shape=(
            shape((devices, rows, 2 * HD), BF16),
            shape((rows, HQ * HD), BF16),
            shape((rows, HQ * HD), BF16),
        ),
        in_specs=[VMEM] * 6,
        out_specs=(VMEM, HBM, HBM),
        scratch_shapes=[
            pltpu.VMEM((2 * LANES, HD), BF16),
            pltpu.VMEM((2 * LANES, HD), BF16),
            pltpu.VMEM((2, HD, LANES), BF16),
            pltpu.VMEM((2, HD, LANES), BF16),
            pltpu.VMEM((total, HD), BF16),
            pltpu.VMEM((total, HD), BF16),
            pltpu.VMEM((WINDOW, LANES), F32),
            pltpu.VMEM((WINDOW, LANES), F32),
            pltpu.VMEM((total, HD), F32),
            pltpu.VMEM((total, HD), F32),
            pltpu.VMEM((rows, HQ * HD), BF16),
            pltpu.VMEM((rows, HQ * HD), BF16),
            pltpu.SemaphoreType.DMA((2, 2)),
        ],
        compiler_params=params(24),
        name="attention",
    )(facts, kv, cosine, sine, queries, out_grad)
    parts = lax.all_to_all(part, "cp", 0, 0, tiled=True)
    grad_keys, grad_values = pl.pallas_call(
        sums_kernel,
        out_shape=(shape((rows, HD), BF16), shape((rows, HD), BF16)),
        in_specs=[VMEM] * 3,
        out_specs=(VMEM, VMEM),
        compiler_params=params(16),
        name="sums",
    )(parts, cosine, sine)
    return attn_out, grad_queries, grad_keys, grad_values


def solution(mesh):
    split = P(("seq", "cp"), None)
    return jax.shard_map(
        shards,
        mesh=mesh,
        in_specs=(split, split, split, split, P(None, "seq"), P("seq"), P("seq")),
        out_specs=(split, split, split, split),
        check_vma=False,
    )
```

```python
import math

import jax
import jax.numpy as jnp
from jax import lax
from jax.experimental import pallas as pl
from jax.experimental.pallas import tpu as pltpu
from jax.sharding import PartitionSpec as P

HQ = 6
HD = 128
HALF = HD // 2
SEC_T = 16
SEC_H = 24
STRETCH = 64
DOCS = 8
WINDOW = 1024 + STRETCH
SUB = 32
LANES = HQ * STRETCH
SCALE = 1.0 / math.sqrt(HD)
LOG2E = math.log2(math.e)
GATHER_ORDER = tuple(range(15, -1, -1))
SCATTER_ORDER = tuple(range(15, -1, -1))

F32 = jnp.float32
BF16 = jnp.bfloat16


def dot_nt(left, right):
    return lax.dot_general(left, right, (((1,), (1,)), ((), ())), preferred_element_type=F32)


def dot_tn(left, right):
    return lax.dot_general(left, right, (((0,), (0,)), ((), ())), preferred_element_type=F32)


def dot_nn(left, right):
    return lax.dot_general(left, right, (((1,), (0,)), ((), ())), preferred_element_type=F32)


def rotated(x, cosine, signed_sine):
    return x * cosine + pltpu.roll(x, HALF, 1) * signed_sine


def rotated_back(x, cosine, signed_sine):
    return x * cosine - pltpu.roll(x, HALF, 1) * signed_sine


def prepare_kernel(
    order_ref, keys_ref, values_ref, pos_ref, docs_ref, payload_ref, cos_ref, sin_ref, facts_ref
):
    me = lax.axis_index("cp")
    rows = keys_ref.shape[0]
    lane = lax.broadcasted_iota(jnp.int32, (1, rows), 1)
    windows = []
    for place in range(2):
        stretch = order_ref[2 * me + place]
        start = pl.multiple_of((stretch // 2) * 128, 128)
        window = pos_ref[:, pl.ds(start, 128)].astype(F32)
        turned = pltpu.roll(window, HALF, 1)
        windows.append(jnp.where(stretch % 2 == place, window, turned))
    pos = jnp.where(lane < STRETCH, windows[0], windows[1])
    pair = lax.broadcasted_iota(jnp.int32, (HALF, 1), 0)
    freq = jnp.exp(-(2.0 * pair.astype(F32) / HD) * math.log(1000000.0))
    chosen = jnp.where(
        pair < SEC_T, pos[0:1, :], jnp.where(pair < SEC_T + SEC_H, pos[1:2, :], pos[2:3, :])
    )
    angle = chosen * freq
    table = jnp.concatenate([jnp.cos(angle), jnp.sin(angle)], axis=0).T
    other = pltpu.roll(table, HALF, 1)
    column = lax.broadcasted_iota(jnp.int32, (1, HD), 1)
    cosine = jnp.where(column < HALF, table, other)
    signed_sine = jnp.where(column < HALF, -other, table)
    cos_ref[...] = cosine
    sin_ref[...] = signed_sine
    k_rot = rotated(keys_ref[...].astype(F32), cosine, signed_sine).astype(BF16)
    values = values_ref[...]
    for peer in range(payload_ref.shape[0]):
        payload_ref[peer, :, :HD] = k_rot
        payload_ref[peer, :, HD:] = values
    docs = docs_ref[...]
    starts = [jnp.sum((docs < doc).astype(jnp.int32)) for doc in range(DOCS)]
    lanes = lax.broadcasted_iota(jnp.int32, (1, 128), 1)
    order = jnp.zeros((1, 128), jnp.int32)
    for block in range(order_ref.shape[0]):
        order = jnp.where(lanes == block, order_ref[block], order)
    firsts = [order_ref[2 * me + place] * STRETCH for place in range(2)]
    facts_ref[0:1, :] = order
    facts_ref[1:2, :] = jnp.where(lanes == 0, firsts[0], firsts[1])
    for place, first in enumerate(firsts):
        token = first + lanes % STRETCH
        low = jnp.zeros((1, 128), jnp.int32)
        for start in starts:
            low = jnp.where(start <= token, jnp.maximum(low, start), low)
        facts_ref[2 + place : 3 + place, :] = low
        facts_ref[4 + place : 5 + place, :] = token


def attention_kernel(
    facts_ref, kv_ref, cos_ref, sin_ref, queries_ref, grad_ref,
    part_ref, out_ref, dq_ref,
    q_ref, do_ref, q_t_ref, do_t_ref, k_seq, v_seq, e_buf, dp_buf, dk_acc, dv_acc, out_buf, dq_buf, sems,
):
    cosine, signed_sine = cos_ref[...], sin_ref[...]
    for place in range(2):
        part = slice(place * STRETCH, (place + 1) * STRETCH)
        for head in range(HQ):
            cols = slice(head * HD, (head + 1) * HD)
            to = pl.ds(place * LANES + head * STRETCH, STRETCH)
            q_ref[to, :] = rotated(
                queries_ref[part, cols].astype(F32), cosine[part], signed_sine[part]
            ).astype(BF16)
            do_ref[to, :] = grad_ref[part, cols]
        half = pl.ds(place * LANES, LANES)
        q_t_ref[place] = q_ref[half, :].T
        do_t_ref[place] = do_ref[half, :].T
    blocks = k_seq.shape[0] // STRETCH
    for block in range(blocks):
        to = pl.ds(pl.multiple_of(facts_ref[0, block] * STRETCH, STRETCH), STRETCH)
        rows = pl.ds((block % 2) * STRETCH, STRETCH)
        peer = GATHER_ORDER.index(block // 2)
        k_seq[to, :] = kv_ref[peer, rows, :HD]
        v_seq[to, :] = kv_ref[peer, rows, HD:]
    dk_acc[...] = jnp.zeros_like(dk_acc)
    dv_acc[...] = jnp.zeros_like(dv_acc)
    tiles = [slice(j * 128, (j + 1) * 128) for j in range(LANES // 128)]
    steps = range(0, WINDOW, SUB)
    down = lax.broadcasted_iota(jnp.int32, (SUB, 128), 0)
    factor = SCALE * LOG2E

    def folded(x, how):
        return how(x.reshape(SUB // 8, 8, 128), axis=0)

    def one_stretch(place, carry):
        first = jnp.where(place == 0, facts_ref[1, 0], facts_ref[1, 1])
        low = facts_ref[pl.ds(2 + place, 1), :]
        token = facts_ref[pl.ds(4 + place, 1), :]
        base = pl.multiple_of(jnp.maximum(first + STRETCH - WINDOW, 0), STRETCH)
        window = pl.ds(base, WINDOW)
        mine = pl.ds(pl.multiple_of(place * LANES, LANES), LANES)

        s = dot_nn(k_seq[window, :], q_t_ref[place])
        tops = [jnp.full((8, 128), -jnp.inf, F32) for _ in tiles]
        for r in steps:
            key = down + (base + r)
            allowed = (key >= low) & (key <= token)
            for j, cols in enumerate(tiles):
                x = jnp.where(allowed, s[r : r + SUB, cols], -jnp.inf)
                e_buf[r : r + SUB, cols] = x
                tops[j] = jnp.maximum(tops[j], folded(x, jnp.max))
        tops = [jnp.max(t, axis=0, keepdims=True) * factor for t in tops]

        dp = dot_nn(v_seq[window, :], do_t_ref[place])
        totals = [jnp.zeros((8, 128), F32) for _ in tiles]
        deltas = [jnp.zeros((8, 128), F32) for _ in tiles]
        for r in steps:
            for j, cols in enumerate(tiles):
                e = jnp.exp2(e_buf[r : r + SUB, cols] * factor - tops[j])
                d = dp[r : r + SUB, cols]
                e_buf[r : r + SUB, cols] = e
                dp_buf[r : r + SUB, cols] = d
                totals[j] = totals[j] + folded(e, jnp.sum)
                deltas[j] = deltas[j] + folded(e * d, jnp.sum)
        inverse = [1.0 / jnp.sum(t, axis=0, keepdims=True) for t in totals]
        deltas = [jnp.sum(d, axis=0, keepdims=True) * i for d, i in zip(deltas, inverse)]

        p_cols, ds_cols = [], []
        for j, cols in enumerate(tiles):
            p_rows, ds_rows = [], []
            for r in steps:
                p = e_buf[r : r + SUB, cols] * inverse[j]
                p_rows.append(p.astype(BF16))
                ds_rows.append((p * (dp_buf[r : r + SUB, cols] - deltas[j])).astype(BF16))
            p_cols.append(jnp.concatenate(p_rows, axis=0))
            ds_cols.append(jnp.concatenate(ds_rows, axis=0))
        p = jnp.concatenate(p_cols, axis=1)
        ds = jnp.concatenate(ds_cols, axis=1)
        out = dot_tn(v_seq[window, :], p).T
        dq = dot_tn(k_seq[window, :], ds).T * SCALE
        rows = pl.ds(pl.multiple_of(place * STRETCH, STRETCH), STRETCH)
        cosine, signed_sine = cos_ref[rows, :], sin_ref[rows, :]
        for head in range(HQ):
            cols = slice(head * HD, (head + 1) * HD)
            part = slice(head * STRETCH, (head + 1) * STRETCH)
            out_buf[rows, cols] = out[part].astype(BF16)
            dq_buf[rows, cols] = rotated_back(dq[part], cosine, signed_sine).astype(BF16)
        for copy in results(place):
            copy.start()
        dv_acc[window, :] += dot_nn(p, do_ref[mine, :])
        dk_acc[window, :] += dot_nn(ds, q_ref[mine, :])
        return carry

    def results(place):
        rows = pl.ds(pl.multiple_of(place * STRETCH, STRETCH), STRETCH)
        return (
            pltpu.make_async_copy(out_buf.at[rows], out_ref.at[rows], sems.at[0, place]),
            pltpu.make_async_copy(dq_buf.at[rows], dq_ref.at[rows], sems.at[1, place]),
        )

    lax.fori_loop(0, 2, one_stretch, 0)
    for block in range(blocks):
        at = pl.ds(pl.multiple_of(facts_ref[0, block] * STRETCH, STRETCH), STRETCH)
        rows = pl.ds((block % 2) * STRETCH, STRETCH)
        peer = SCATTER_ORDER.index(block // 2)
        part_ref[peer, rows, :HD] = (dk_acc[at, :] * SCALE).astype(BF16)
        part_ref[peer, rows, HD:] = dv_acc[at, :].astype(BF16)
    for place in range(2):
        for copy in results(place):
            copy.wait()


def sums_kernel(parts_ref, cos_ref, sin_ref, dk_ref, dv_ref):
    total = parts_ref[0].astype(F32)
    for peer in range(1, parts_ref.shape[0]):
        total = total + parts_ref[peer].astype(F32)
    dk_ref[...] = rotated_back(total[:, :HD], cos_ref[...], sin_ref[...]).astype(BF16)
    dv_ref[...] = total[:, HD:].astype(BF16)


def in_hbm(x):
    return pltpu.with_memory_space_constraint(x, pltpu.HBM)


def params(mib):
    return pltpu.CompilerParams(vmem_limit_bytes=mib * 2**20)


VMEM = pl.BlockSpec(memory_space=pltpu.VMEM)
HBM = pl.BlockSpec(memory_space=pltpu.HBM)
SMEM = pl.BlockSpec(memory_space=pltpu.SMEM)


def exchanged(blocks, order):
    return lax.all_to_all(blocks, "cp", 0, 0, axis_index_groups=[list(order)], tiled=True)


def shards(queries, keys, values, out_grad, positions, doc_ids, stretch_order):
    devices = lax.axis_size("cp")
    rows = queries.shape[0]
    total = rows * devices
    shape = jax.ShapeDtypeStruct
    docs = doc_ids.reshape(total // 128, 128)
    payload, cosine, sine, facts = pl.pallas_call(
        prepare_kernel,
        out_shape=(
            shape((devices, rows, 2 * HD), BF16),
            shape((rows, HD), F32),
            shape((rows, HD), F32),
            shape((8, 128), jnp.int32),
        ),
        in_specs=[SMEM] + [VMEM] * 4,
        out_specs=(VMEM,) * 4,
        compiler_params=params(16),
        name="prepare",
    )(
        *(in_hbm(x) for x in (stretch_order, keys, values, positions, docs)),
    )
    kv = exchanged(payload, GATHER_ORDER)
    part, attn_out, grad_queries = pl.pallas_call(
        attention_kernel,
        out_shape=(
            shape((devices, rows, 2 * HD), BF16),
            shape((rows, HQ * HD), BF16),
            shape((rows, HQ * HD), BF16),
        ),
        in_specs=[VMEM] * 6,
        out_specs=(VMEM, HBM, HBM),
        scratch_shapes=[
            pltpu.VMEM((2 * LANES, HD), BF16),
            pltpu.VMEM((2 * LANES, HD), BF16),
            pltpu.VMEM((2, HD, LANES), BF16),
            pltpu.VMEM((2, HD, LANES), BF16),
            pltpu.VMEM((total, HD), BF16),
            pltpu.VMEM((total, HD), BF16),
            pltpu.VMEM((WINDOW, LANES), F32),
            pltpu.VMEM((WINDOW, LANES), F32),
            pltpu.VMEM((total, HD), F32),
            pltpu.VMEM((total, HD), F32),
            pltpu.VMEM((rows, HQ * HD), BF16),
            pltpu.VMEM((rows, HQ * HD), BF16),
            pltpu.SemaphoreType.DMA((2, 2)),
        ],
        compiler_params=params(24),
        name="attention",
    )(facts, kv, cosine, sine, queries, out_grad)
    parts = exchanged(part, SCATTER_ORDER)
    grad_keys, grad_values = pl.pallas_call(
        sums_kernel,
        out_shape=(shape((rows, HD), BF16), shape((rows, HD), BF16)),
        in_specs=[VMEM] * 3,
        out_specs=(VMEM, VMEM),
        compiler_params=params(16),
        name="sums",
    )(parts, cosine, sine)
    return attn_out, grad_queries, grad_keys, grad_values


def solution(mesh):
    split = P(("seq", "cp"), None)
    return jax.shard_map(
        shards,
        mesh=mesh,
        in_specs=(split, split, split, split, P(None, "seq"), P("seq"), P("seq")),
        out_specs=(split, split, split, split),
        check_vma=False,
    )
```

```python
import math

import jax
import jax.numpy as jnp
from jax import lax
from jax.experimental import pallas as pl
from jax.experimental.pallas import tpu as pltpu
from jax.sharding import PartitionSpec as P

HQ = 6
HD = 128
HALF = HD // 2
SEC_T = 16
SEC_H = 24
STRETCH = 64
DOCS = 8
WINDOW = 1024 + STRETCH
SUB = 32
LANES = HQ * STRETCH
SCALE = 1.0 / math.sqrt(HD)
LOG2E = math.log2(math.e)
GATHER_ORDER = (11, 15, 9, 1, 12, 2, 14, 10, 0, 4, 7, 6, 13, 5, 3, 8)
SCATTER_ORDER = tuple(range(15, -1, -1))

F32 = jnp.float32
BF16 = jnp.bfloat16


def dot_nt(left, right):
    return lax.dot_general(left, right, (((1,), (1,)), ((), ())), preferred_element_type=F32)


def dot_tn(left, right):
    return lax.dot_general(left, right, (((0,), (0,)), ((), ())), preferred_element_type=F32)


def dot_nn(left, right):
    return lax.dot_general(left, right, (((1,), (0,)), ((), ())), preferred_element_type=F32)


def rotated(x, cosine, signed_sine):
    return x * cosine + pltpu.roll(x, HALF, 1) * signed_sine


def rotated_back(x, cosine, signed_sine):
    return x * cosine - pltpu.roll(x, HALF, 1) * signed_sine


def prepare_kernel(
    order_ref, keys_ref, values_ref, pos_ref, docs_ref, payload_ref, cos_ref, sin_ref, facts_ref
):
    me = lax.axis_index("cp")
    rows = keys_ref.shape[0]
    lane = lax.broadcasted_iota(jnp.int32, (1, rows), 1)
    windows = []
    for place in range(2):
        stretch = order_ref[2 * me + place]
        start = pl.multiple_of((stretch // 2) * 128, 128)
        window = pos_ref[:, pl.ds(start, 128)].astype(F32)
        turned = pltpu.roll(window, HALF, 1)
        windows.append(jnp.where(stretch % 2 == place, window, turned))
    pos = jnp.where(lane < STRETCH, windows[0], windows[1])
    pair = lax.broadcasted_iota(jnp.int32, (HALF, 1), 0)
    freq = jnp.exp(-(2.0 * pair.astype(F32) / HD) * math.log(1000000.0))
    chosen = jnp.where(
        pair < SEC_T, pos[0:1, :], jnp.where(pair < SEC_T + SEC_H, pos[1:2, :], pos[2:3, :])
    )
    angle = chosen * freq
    table = jnp.concatenate([jnp.cos(angle), jnp.sin(angle)], axis=0).T
    other = pltpu.roll(table, HALF, 1)
    column = lax.broadcasted_iota(jnp.int32, (1, HD), 1)
    cosine = jnp.where(column < HALF, table, other)
    signed_sine = jnp.where(column < HALF, -other, table)
    cos_ref[...] = cosine
    sin_ref[...] = signed_sine
    k_rot = rotated(keys_ref[...].astype(F32), cosine, signed_sine).astype(BF16)
    values = values_ref[...]
    for peer in range(payload_ref.shape[0]):
        payload_ref[peer, :, :HD] = k_rot
        payload_ref[peer, :, HD:] = values
    docs = docs_ref[...]
    starts = [jnp.sum((docs < doc).astype(jnp.int32)) for doc in range(DOCS)]
    lanes = lax.broadcasted_iota(jnp.int32, (1, 128), 1)
    order = jnp.zeros((1, 128), jnp.int32)
    for block in range(order_ref.shape[0]):
        order = jnp.where(lanes == block, order_ref[block], order)
    firsts = [order_ref[2 * me + place] * STRETCH for place in range(2)]
    facts_ref[0:1, :] = order
    facts_ref[1:2, :] = jnp.where(lanes == 0, firsts[0], firsts[1])
    for place, first in enumerate(firsts):
        token = first + lanes % STRETCH
        low = jnp.zeros((1, 128), jnp.int32)
        for start in starts:
            low = jnp.where(start <= token, jnp.maximum(low, start), low)
        facts_ref[2 + place : 3 + place, :] = low
        facts_ref[4 + place : 5 + place, :] = token


def attention_kernel(
    facts_ref, kv_ref, cos_ref, sin_ref, queries_ref, grad_ref,
    part_ref, out_ref, dq_ref,
    q_ref, do_ref, q_t_ref, do_t_ref, k_seq, v_seq, e_buf, dp_buf, dk_acc, dv_acc, out_buf, dq_buf, sems,
):
    cosine, signed_sine = cos_ref[...], sin_ref[...]
    for place in range(2):
        part = slice(place * STRETCH, (place + 1) * STRETCH)
        for head in range(HQ):
            cols = slice(head * HD, (head + 1) * HD)
            to = pl.ds(place * LANES + head * STRETCH, STRETCH)
            q_ref[to, :] = rotated(
                queries_ref[part, cols].astype(F32), cosine[part], signed_sine[part]
            ).astype(BF16)
            do_ref[to, :] = grad_ref[part, cols]
        half = pl.ds(place * LANES, LANES)
        q_t_ref[place] = q_ref[half, :].T
        do_t_ref[place] = do_ref[half, :].T
    blocks = k_seq.shape[0] // STRETCH
    for block in range(blocks):
        to = pl.ds(pl.multiple_of(facts_ref[0, block] * STRETCH, STRETCH), STRETCH)
        rows = pl.ds((block % 2) * STRETCH, STRETCH)
        peer = GATHER_ORDER.index(block // 2)
        k_seq[to, :] = kv_ref[peer, rows, :HD]
        v_seq[to, :] = kv_ref[peer, rows, HD:]
    dk_acc[...] = jnp.zeros_like(dk_acc)
    dv_acc[...] = jnp.zeros_like(dv_acc)
    tiles = [slice(j * 128, (j + 1) * 128) for j in range(LANES // 128)]
    steps = range(0, WINDOW, SUB)
    down = lax.broadcasted_iota(jnp.int32, (SUB, 128), 0)
    factor = SCALE * LOG2E

    def folded(x, how):
        return how(x.reshape(SUB // 8, 8, 128), axis=0)

    def one_stretch(place, carry):
        first = jnp.where(place == 0, facts_ref[1, 0], facts_ref[1, 1])
        low = facts_ref[pl.ds(2 + place, 1), :]
        token = facts_ref[pl.ds(4 + place, 1), :]
        base = pl.multiple_of(jnp.maximum(first + STRETCH - WINDOW, 0), STRETCH)
        window = pl.ds(base, WINDOW)
        mine = pl.ds(pl.multiple_of(place * LANES, LANES), LANES)

        s = dot_nn(k_seq[window, :], q_t_ref[place])
        tops = [jnp.full((8, 128), -jnp.inf, F32) for _ in tiles]
        for r in steps:
            key = down + (base + r)
            allowed = (key >= low) & (key <= token)
            for j, cols in enumerate(tiles):
                x = jnp.where(allowed, s[r : r + SUB, cols], -jnp.inf)
                e_buf[r : r + SUB, cols] = x
                tops[j] = jnp.maximum(tops[j], folded(x, jnp.max))
        tops = [jnp.max(t, axis=0, keepdims=True) * factor for t in tops]

        dp = dot_nn(v_seq[window, :], do_t_ref[place])
        totals = [jnp.zeros((8, 128), F32) for _ in tiles]
        deltas = [jnp.zeros((8, 128), F32) for _ in tiles]
        for r in steps:
            for j, cols in enumerate(tiles):
                e = jnp.exp2(e_buf[r : r + SUB, cols] * factor - tops[j])
                d = dp[r : r + SUB, cols]
                e_buf[r : r + SUB, cols] = e
                dp_buf[r : r + SUB, cols] = d
                totals[j] = totals[j] + folded(e, jnp.sum)
                deltas[j] = deltas[j] + folded(e * d, jnp.sum)
        inverse = [1.0 / jnp.sum(t, axis=0, keepdims=True) for t in totals]
        deltas = [jnp.sum(d, axis=0, keepdims=True) * i for d, i in zip(deltas, inverse)]

        p_cols, ds_cols = [], []
        for j, cols in enumerate(tiles):
            p_rows, ds_rows = [], []
            for r in steps:
                p = e_buf[r : r + SUB, cols] * inverse[j]
                p_rows.append(p.astype(BF16))
                ds_rows.append((p * (dp_buf[r : r + SUB, cols] - deltas[j])).astype(BF16))
            p_cols.append(jnp.concatenate(p_rows, axis=0))
            ds_cols.append(jnp.concatenate(ds_rows, axis=0))
        p = jnp.concatenate(p_cols, axis=1)
        ds = jnp.concatenate(ds_cols, axis=1)
        out = dot_tn(v_seq[window, :], p).T
        dq = dot_tn(k_seq[window, :], ds).T * SCALE
        rows = pl.ds(pl.multiple_of(place * STRETCH, STRETCH), STRETCH)
        cosine, signed_sine = cos_ref[rows, :], sin_ref[rows, :]
        for head in range(HQ):
            cols = slice(head * HD, (head + 1) * HD)
            part = slice(head * STRETCH, (head + 1) * STRETCH)
            out_buf[rows, cols] = out[part].astype(BF16)
            dq_buf[rows, cols] = rotated_back(dq[part], cosine, signed_sine).astype(BF16)
        for copy in results(place):
            copy.start()
        dv_acc[window, :] += dot_nn(p, do_ref[mine, :])
        dk_acc[window, :] += dot_nn(ds, q_ref[mine, :])
        return carry

    def results(place):
        rows = pl.ds(pl.multiple_of(place * STRETCH, STRETCH), STRETCH)
        return (
            pltpu.make_async_copy(out_buf.at[rows], out_ref.at[rows], sems.at[0, place]),
            pltpu.make_async_copy(dq_buf.at[rows], dq_ref.at[rows], sems.at[1, place]),
        )

    lax.fori_loop(0, 2, one_stretch, 0)
    for block in range(blocks):
        at = pl.ds(pl.multiple_of(facts_ref[0, block] * STRETCH, STRETCH), STRETCH)
        rows = pl.ds((block % 2) * STRETCH, STRETCH)
        peer = SCATTER_ORDER.index(block // 2)
        part_ref[peer, rows, :HD] = (dk_acc[at, :] * SCALE).astype(BF16)
        part_ref[peer, rows, HD:] = dv_acc[at, :].astype(BF16)
    for place in range(2):
        for copy in results(place):
            copy.wait()


def sums_kernel(parts_ref, cos_ref, sin_ref, dk_ref, dv_ref):
    total = parts_ref[0].astype(F32)
    for peer in range(1, parts_ref.shape[0]):
        total = total + parts_ref[peer].astype(F32)
    dk_ref[...] = rotated_back(total[:, :HD], cos_ref[...], sin_ref[...]).astype(BF16)
    dv_ref[...] = total[:, HD:].astype(BF16)


def in_hbm(x):
    return pltpu.with_memory_space_constraint(x, pltpu.HBM)


def params(mib):
    return pltpu.CompilerParams(vmem_limit_bytes=mib * 2**20)


VMEM = pl.BlockSpec(memory_space=pltpu.VMEM)
HBM = pl.BlockSpec(memory_space=pltpu.HBM)
SMEM = pl.BlockSpec(memory_space=pltpu.SMEM)


def exchanged(blocks, order):
    return lax.all_to_all(blocks, "cp", 0, 0, axis_index_groups=[list(order)], tiled=True)


def shards(queries, keys, values, out_grad, positions, doc_ids, stretch_order):
    devices = lax.axis_size("cp")
    rows = queries.shape[0]
    total = rows * devices
    shape = jax.ShapeDtypeStruct
    docs = doc_ids.reshape(total // 128, 128)
    payload, cosine, sine, facts = pl.pallas_call(
        prepare_kernel,
        out_shape=(
            shape((devices, rows, 2 * HD), BF16),
            shape((rows, HD), F32),
            shape((rows, HD), F32),
            shape((8, 128), jnp.int32),
        ),
        in_specs=[SMEM] + [VMEM] * 4,
        out_specs=(VMEM,) * 4,
        compiler_params=params(16),
        name="prepare",
    )(
        *(in_hbm(x) for x in (stretch_order, keys, values, positions, docs)),
    )
    kv = exchanged(payload, GATHER_ORDER)
    part, attn_out, grad_queries = pl.pallas_call(
        attention_kernel,
        out_shape=(
            shape((devices, rows, 2 * HD), BF16),
            shape((rows, HQ * HD), BF16),
            shape((rows, HQ * HD), BF16),
        ),
        in_specs=[VMEM] * 6,
        out_specs=(VMEM, HBM, HBM),
        scratch_shapes=[
            pltpu.VMEM((2 * LANES, HD), BF16),
            pltpu.VMEM((2 * LANES, HD), BF16),
            pltpu.VMEM((2, HD, LANES), BF16),
            pltpu.VMEM((2, HD, LANES), BF16),
            pltpu.VMEM((total, HD), BF16),
            pltpu.VMEM((total, HD), BF16),
            pltpu.VMEM((WINDOW, LANES), F32),
            pltpu.VMEM((WINDOW, LANES), F32),
            pltpu.VMEM((total, HD), F32),
            pltpu.VMEM((total, HD), F32),
            pltpu.VMEM((rows, HQ * HD), BF16),
            pltpu.VMEM((rows, HQ * HD), BF16),
            pltpu.SemaphoreType.DMA((2, 2)),
        ],
        compiler_params=params(24),
        name="attention",
    )(facts, kv, cosine, sine, queries, out_grad)
    parts = exchanged(part, SCATTER_ORDER)
    grad_keys, grad_values = pl.pallas_call(
        sums_kernel,
        out_shape=(shape((rows, HD), BF16), shape((rows, HD), BF16)),
        in_specs=[VMEM] * 3,
        out_specs=(VMEM, VMEM),
        compiler_params=params(16),
        name="sums",
    )(parts, cosine, sine)
    return attn_out, grad_queries, grad_keys, grad_values


def solution(mesh):
    split = P(("seq", "cp"), None)
    return jax.shard_map(
        shards,
        mesh=mesh,
        in_specs=(split, split, split, split, P(None, "seq"), P("seq"), P("seq")),
        out_specs=(split, split, split, split),
        check_vma=False,
    )
```

```python
import math

import jax
import jax.numpy as jnp
from jax import lax
from jax.experimental import pallas as pl
from jax.experimental.pallas import tpu as pltpu
from jax.sharding import PartitionSpec as P

HQ = 6
HD = 128
HALF = HD // 2
SEC_T = 16
SEC_H = 24
STRETCH = 64
DOCS = 8
WINDOW = 1024 + STRETCH
SUB = 32
LANES = HQ * STRETCH
SCALE = 1.0 / math.sqrt(HD)
LOG2E = math.log2(math.e)
GATHER_ORDER = tuple(range(15, -1, -1))
SCATTER_ORDER = tuple(range(15, -1, -1))

F32 = jnp.float32
BF16 = jnp.bfloat16


def dot_nt(left, right):
    return lax.dot_general(left, right, (((1,), (1,)), ((), ())), preferred_element_type=F32)


def dot_tn(left, right):
    return lax.dot_general(left, right, (((0,), (0,)), ((), ())), preferred_element_type=F32)


def dot_nn(left, right):
    return lax.dot_general(left, right, (((1,), (0,)), ((), ())), preferred_element_type=F32)


def rotated(x, cosine, signed_sine):
    return x * cosine + pltpu.roll(x, HALF, 1) * signed_sine


def rotated_back(x, cosine, signed_sine):
    return x * cosine - pltpu.roll(x, HALF, 1) * signed_sine


def prepare_kernel(
    order_ref, keys_ref, values_ref, pos_ref, docs_ref, payload_ref, cos_ref, sin_ref, facts_ref
):
    me = lax.axis_index("cp")
    rows = keys_ref.shape[0]
    lane = lax.broadcasted_iota(jnp.int32, (1, rows), 1)
    windows = []
    for place in range(2):
        stretch = order_ref[2 * me + place]
        start = pl.multiple_of((stretch // 2) * 128, 128)
        window = pos_ref[:, pl.ds(start, 128)].astype(F32)
        turned = pltpu.roll(window, HALF, 1)
        windows.append(jnp.where(stretch % 2 == place, window, turned))
    pos = jnp.where(lane < STRETCH, windows[0], windows[1])
    pair = lax.broadcasted_iota(jnp.int32, (HALF, 1), 0)
    freq = jnp.exp(-(2.0 * pair.astype(F32) / HD) * math.log(1000000.0))
    chosen = jnp.where(
        pair < SEC_T, pos[0:1, :], jnp.where(pair < SEC_T + SEC_H, pos[1:2, :], pos[2:3, :])
    )
    angle = chosen * freq
    table = jnp.concatenate([jnp.cos(angle), jnp.sin(angle)], axis=0).T
    other = pltpu.roll(table, HALF, 1)
    column = lax.broadcasted_iota(jnp.int32, (1, HD), 1)
    cosine = jnp.where(column < HALF, table, other)
    signed_sine = jnp.where(column < HALF, -other, table)
    cos_ref[...] = cosine
    sin_ref[...] = signed_sine
    k_rot = rotated(keys_ref[...].astype(F32), cosine, signed_sine).astype(BF16)
    values = values_ref[...]
    for peer in range(payload_ref.shape[0]):
        payload_ref[peer, :, :HD] = k_rot
        payload_ref[peer, :, HD:] = values
    docs = docs_ref[...]
    starts = [jnp.sum((docs < doc).astype(jnp.int32)) for doc in range(DOCS)]
    lanes = lax.broadcasted_iota(jnp.int32, (1, 128), 1)
    order = jnp.zeros((1, 128), jnp.int32)
    for block in range(order_ref.shape[0]):
        order = jnp.where(lanes == block, order_ref[block], order)
    firsts = [order_ref[2 * me + place] * STRETCH for place in range(2)]
    facts_ref[0:1, :] = order
    facts_ref[1:2, :] = jnp.where(lanes == 0, firsts[0], firsts[1])
    for place, first in enumerate(firsts):
        token = first + lanes % STRETCH
        low = jnp.zeros((1, 128), jnp.int32)
        for start in starts:
            low = jnp.where(start <= token, jnp.maximum(low, start), low)
        facts_ref[2 + place : 3 + place, :] = low
        facts_ref[4 + place : 5 + place, :] = token


def attention_kernel(
    facts_ref, kv_ref, cos_ref, sin_ref, queries_ref, grad_ref,
    part_ref, out_ref, dq_ref,
    q_ref, do_ref, q_t_ref, do_t_ref, k_seq, v_seq, e_buf, dp_buf, dk_acc, dv_acc, out_buf, dq_buf, sems,
):
    cosine, signed_sine = cos_ref[...], sin_ref[...]
    for place in range(2):
        part = slice(place * STRETCH, (place + 1) * STRETCH)
        for head in range(HQ):
            cols = slice(head * HD, (head + 1) * HD)
            to = pl.ds(place * LANES + head * STRETCH, STRETCH)
            q_ref[to, :] = rotated(
                queries_ref[part, cols].astype(F32), cosine[part], signed_sine[part]
            ).astype(BF16)
            do_ref[to, :] = grad_ref[part, cols]
        half = pl.ds(place * LANES, LANES)
        q_t_ref[place] = q_ref[half, :].T
        do_t_ref[place] = do_ref[half, :].T
    blocks = k_seq.shape[0] // STRETCH
    for block in range(blocks):
        to = pl.ds(pl.multiple_of(facts_ref[0, block] * STRETCH, STRETCH), STRETCH)
        rows = pl.ds((block % 2) * STRETCH, STRETCH)
        peer = GATHER_ORDER.index(block // 2)
        k_seq[to, :] = kv_ref[peer, rows, :HD]
        v_seq[to, :] = kv_ref[peer, rows, HD:]
    dk_acc[...] = jnp.zeros_like(dk_acc)
    dv_acc[...] = jnp.zeros_like(dv_acc)
    tiles = [slice(j * 128, (j + 1) * 128) for j in range(LANES // 128)]
    steps = range(0, WINDOW, SUB)
    down = lax.broadcasted_iota(jnp.int32, (SUB, 128), 0)
    factor = SCALE * LOG2E

    def folded(x, how):
        return how(x.reshape(SUB // 8, 8, 128), axis=0)

    def one_stretch(place, carry):
        first = jnp.where(place == 0, facts_ref[1, 0], facts_ref[1, 1])
        low = facts_ref[pl.ds(2 + place, 1), :]
        token = facts_ref[pl.ds(4 + place, 1), :]
        base = pl.multiple_of(jnp.maximum(first + STRETCH - WINDOW, 0), STRETCH)
        window = pl.ds(base, WINDOW)
        mine = pl.ds(pl.multiple_of(place * LANES, LANES), LANES)

        s = dot_nn(k_seq[window, :], q_t_ref[place])
        tops = [jnp.full((8, 128), -jnp.inf, F32) for _ in tiles]
        for r in steps:
            key = down + (base + r)
            allowed = (key >= low) & (key <= token)
            for j, cols in enumerate(tiles):
                x = jnp.where(allowed, s[r : r + SUB, cols], -jnp.inf)
                e_buf[r : r + SUB, cols] = x
                tops[j] = jnp.maximum(tops[j], folded(x, jnp.max))
        tops = [jnp.max(t, axis=0, keepdims=True) * factor for t in tops]

        dp = dot_nn(v_seq[window, :], do_t_ref[place])
        totals = [jnp.zeros((8, 128), F32) for _ in tiles]
        deltas = [jnp.zeros((8, 128), F32) for _ in tiles]
        for r in steps:
            for j, cols in enumerate(tiles):
                e = jnp.exp2(e_buf[r : r + SUB, cols] * factor - tops[j])
                d = dp[r : r + SUB, cols]
                e_buf[r : r + SUB, cols] = e
                dp_buf[r : r + SUB, cols] = d
                totals[j] = totals[j] + folded(e, jnp.sum)
                deltas[j] = deltas[j] + folded(e * d, jnp.sum)
        inverse = [1.0 / jnp.sum(t, axis=0, keepdims=True) for t in totals]
        deltas = [jnp.sum(d, axis=0, keepdims=True) * i for d, i in zip(deltas, inverse)]

        p_cols, ds_cols = [], []
        for j, cols in enumerate(tiles):
            p_rows, ds_rows = [], []
            for r in steps:
                p = e_buf[r : r + SUB, cols] * inverse[j]
                p_rows.append(p.astype(BF16))
                ds_rows.append((p * (dp_buf[r : r + SUB, cols] - deltas[j])).astype(BF16))
            p_cols.append(jnp.concatenate(p_rows, axis=0))
            ds_cols.append(jnp.concatenate(ds_rows, axis=0))
        p = jnp.concatenate(p_cols, axis=1)
        ds = jnp.concatenate(ds_cols, axis=1)
        out = dot_tn(v_seq[window, :], p).T
        dq = dot_tn(k_seq[window, :], ds).T * SCALE
        rows = pl.ds(pl.multiple_of(place * STRETCH, STRETCH), STRETCH)
        cosine, signed_sine = cos_ref[rows, :], sin_ref[rows, :]
        for head in range(HQ):
            cols = slice(head * HD, (head + 1) * HD)
            part = slice(head * STRETCH, (head + 1) * STRETCH)
            out_buf[rows, cols] = out[part].astype(BF16)
            dq_buf[rows, cols] = rotated_back(dq[part], cosine, signed_sine).astype(BF16)
        for copy in results(place):
            copy.start()
        dv_acc[window, :] += dot_nn(p, do_ref[mine, :])
        dk_acc[window, :] += dot_nn(ds, q_ref[mine, :])
        return carry

    def results(place):
        rows = pl.ds(pl.multiple_of(place * STRETCH, STRETCH), STRETCH)
        return (
            pltpu.make_async_copy(out_buf.at[rows], out_ref.at[rows], sems.at[0, place]),
            pltpu.make_async_copy(dq_buf.at[rows], dq_ref.at[rows], sems.at[1, place]),
        )

    for place in range(2):
        one_stretch(place, 0)
    for block in range(blocks):
        at = pl.ds(pl.multiple_of(facts_ref[0, block] * STRETCH, STRETCH), STRETCH)
        rows = pl.ds((block % 2) * STRETCH, STRETCH)
        peer = SCATTER_ORDER.index(block // 2)
        part_ref[peer, rows, :HD] = (dk_acc[at, :] * SCALE).astype(BF16)
        part_ref[peer, rows, HD:] = dv_acc[at, :].astype(BF16)
    for place in range(2):
        for copy in results(place):
            copy.wait()


def sums_kernel(parts_ref, cos_ref, sin_ref, dk_ref, dv_ref):
    total = parts_ref[0].astype(F32)
    for peer in range(1, parts_ref.shape[0]):
        total = total + parts_ref[peer].astype(F32)
    dk_ref[...] = rotated_back(total[:, :HD], cos_ref[...], sin_ref[...]).astype(BF16)
    dv_ref[...] = total[:, HD:].astype(BF16)


def in_hbm(x):
    return pltpu.with_memory_space_constraint(x, pltpu.HBM)


def params(mib):
    return pltpu.CompilerParams(vmem_limit_bytes=mib * 2**20)


VMEM = pl.BlockSpec(memory_space=pltpu.VMEM)
HBM = pl.BlockSpec(memory_space=pltpu.HBM)
SMEM = pl.BlockSpec(memory_space=pltpu.SMEM)


def exchanged(blocks, order):
    return lax.all_to_all(blocks, "cp", 0, 0, axis_index_groups=[list(order)], tiled=True)


def shards(queries, keys, values, out_grad, positions, doc_ids, stretch_order):
    devices = lax.axis_size("cp")
    rows = queries.shape[0]
    total = rows * devices
    shape = jax.ShapeDtypeStruct
    docs = doc_ids.reshape(total // 128, 128)
    payload, cosine, sine, facts = pl.pallas_call(
        prepare_kernel,
        out_shape=(
            shape((devices, rows, 2 * HD), BF16),
            shape((rows, HD), F32),
            shape((rows, HD), F32),
            shape((8, 128), jnp.int32),
        ),
        in_specs=[SMEM] + [VMEM] * 4,
        out_specs=(VMEM,) * 4,
        compiler_params=params(16),
        name="prepare",
    )(
        *(in_hbm(x) for x in (stretch_order, keys, values, positions, docs)),
    )
    kv = exchanged(payload, GATHER_ORDER)
    part, attn_out, grad_queries = pl.pallas_call(
        attention_kernel,
        out_shape=(
            shape((devices, rows, 2 * HD), BF16),
            shape((rows, HQ * HD), BF16),
            shape((rows, HQ * HD), BF16),
        ),
        in_specs=[VMEM] * 6,
        out_specs=(VMEM, HBM, HBM),
        scratch_shapes=[
            pltpu.VMEM((2 * LANES, HD), BF16),
            pltpu.VMEM((2 * LANES, HD), BF16),
            pltpu.VMEM((2, HD, LANES), BF16),
            pltpu.VMEM((2, HD, LANES), BF16),
            pltpu.VMEM((total, HD), BF16),
            pltpu.VMEM((total, HD), BF16),
            pltpu.VMEM((WINDOW, LANES), F32),
            pltpu.VMEM((WINDOW, LANES), F32),
            pltpu.VMEM((total, HD), F32),
            pltpu.VMEM((total, HD), F32),
            pltpu.VMEM((rows, HQ * HD), BF16),
            pltpu.VMEM((rows, HQ * HD), BF16),
            pltpu.SemaphoreType.DMA((2, 2)),
        ],
        compiler_params=params(24),
        name="attention",
    )(facts, kv, cosine, sine, queries, out_grad)
    parts = exchanged(part, SCATTER_ORDER)
    grad_keys, grad_values = pl.pallas_call(
        sums_kernel,
        out_shape=(shape((rows, HD), BF16), shape((rows, HD), BF16)),
        in_specs=[VMEM] * 3,
        out_specs=(VMEM, VMEM),
        compiler_params=params(16),
        name="sums",
    )(parts, cosine, sine)
    return attn_out, grad_queries, grad_keys, grad_values


def solution(mesh):
    split = P(("seq", "cp"), None)
    return jax.shard_map(
        shards,
        mesh=mesh,
        in_specs=(split, split, split, split, P(None, "seq"), P("seq"), P("seq")),
        out_specs=(split, split, split, split),
        check_vma=False,
    )
```
